32 devices in a mesh: dp: 2 (over y), seq: 4 (over z), tensor: 4 (over x, core).
Axes of the slice: x: 2, y: 2, z: 4, core: 2. Of those that a mesh axis runs over, the one named last changes fastest.
Arguments:
- layer_input: bfloat16 [6, 1024, 2048], P('dp', 'seq'), may hold values from -6 to 6
- lengths: int32 [6], P('dp'), may hold values from 256 to 1024, as said below
- cotangent: bfloat16 [6, 1024, 2048], P('dp', ('seq', 'tensor')), may hold values from -6 to 6
- ln1_gain: bfloat16 [2048], replicated, may hold values from 0.5 to 1.5
- ln1_bias: bfloat16 [2048], replicated, may hold values from -3 to 3
- w_query: bfloat16 [2048, 2048], P(None, 'tensor'), may hold values from -0.125 to 0.125
- b_query: bfloat16 [2048], P('tensor'), may hold values from -3 to 3
- w_kv: bfloat16 [2048, 256], replicated, may hold values from -0.125 to 0.125
- b_value: bfloat16 [128], replicated, may hold values from -3 to 3
- w_out: bfloat16 [2048, 2048], P('tensor'), may hold values from -0.5 to 0.5
- b_out: bfloat16 [2048], replicated, may hold values from -3 to 3
- ln2_gain: bfloat16 [2048], replicated, may hold values from 0.5 to 1.5
- ln2_bias: bfloat16 [2048], replicated, may hold values from -3 to 3
- w_up: bfloat16 [2048, 8192], P(None, 'tensor'), may hold values from -0.125 to 0.125
- b_up: bfloat16 [8192], P('tensor'), may hold values from -3 to 3
- w_down: bfloat16 [8192, 2048], P('tensor'), may hold values from -0.0625 to 0.0625
- b_down: bfloat16 [2048], replicated, may hold values from -3 to 3
Outputs:
- layer_output: bfloat16 [6, 1024, 2048], P('dp', ('seq', 'tensor'))
- input_grad: float32 [6, 1024, 2048], P('dp', ('seq', 'tensor'))
- g_w_query: float32 [2048, 2048], P(('dp', 'seq'), 'tensor')
- g_b_query: float32 [16, 128], P('tensor', ('dp', 'seq'))
- g_w_kv: float32 [2048, 256], P(('dp', 'seq', 'tensor'))
- g_b_value: float32 [128], P(('dp', 'seq', 'tensor'))
- g_w_out: float32 [2048, 2048], P('tensor', ('dp', 'seq'))
- g_w_up: float32 [2048, 8192], P(('dp', 'seq'), 'tensor')
- g_b_up: float32 [64, 128], P('tensor', ('dp', 'seq'))
- g_w_down: float32 [8192, 2048], P('tensor', ('dp', 'seq'))
- g_norms_biases: float32 [6, 2048], P(None, ('dp', 'seq', 'tensor'))
The draws below stay inside these ranges and needn't reach their ends.
Inputs may be any that keep to these rules, and one draw needn't show every extreme that they name: `lengths`: the number of real tokens at the start of each row; the rest of the row is padding.
All inputs are finite; a program needn't handle non-finite values.
Results may differ from the reference program's by a relative error of at most 0.012.
Values may be sent and summed in bfloat16 or wider, within the bound.
A program may use at most 256 MiB of HBM per device.

```python
import math
import jax
import jax.numpy as jnp
from jax import lax

D = 2048
H = 16
HD = 128
FF = 8192
LEN = 1024
ROWS = 6


def draw_lengths(key, part):
    pick_key, order_key = jax.random.split(key)
    lengths_drawn = jax.random.randint(pick_key, (ROWS,), LEN // 4, LEN + 1)
    shuffled = jax.random.permutation(order_key, ROWS)
    row_ids = jnp.arange(ROWS)
    lengths_drawn = jnp.where(row_ids == shuffled[0], LEN, lengths_drawn)
    lengths_drawn = jnp.where(row_ids == shuffled[1], LEN // 4, lengths_drawn)
    return lengths_drawn.astype(jnp.int32)


def strengthened(array, key, source, target, blocks, factor):
    def block_of(dim):
        return (jnp.arange(array.shape[dim]) // (array.shape[dim] // blocks)).reshape((-1,) + (1,) * (array.ndim - 1 - dim))

    first = jax.random.permutation(key, blocks)[block_of(target)]
    second = (block_of(target) + blocks // 2) % blocks
    return jnp.where((block_of(source) == first) | (block_of(source) == second), factor * array, array)


def steps_of(rng, dims, pieces, smallest, high):
    def one(dim, parts):
        heights = jax.random.uniform(jax.random.fold_in(jax.random.fold_in(rng, 6), dim), (parts,), jnp.float32, smallest / len(pieces), high / len(pieces))
        return jnp.repeat(jnp.exp(heights), dims[dim] // parts).reshape((-1,) + (1,) * (len(dims) - dim - 1))

    loudness = one(*pieces[0])
    for cut in pieces[1:]:
        loudness = loudness * one(*cut)
    return loudness


def noise(rng, dims, width, bound, cuts=(), kind=jnp.bfloat16):
    level = steps_of(rng, dims, cuts, -0.22, 0.18) if cuts else 1.0
    entries = jax.random.normal(rng, dims, jnp.float32) * width * level
    return jnp.minimum(jnp.maximum(entries, -bound), bound).astype(kind)


def bell_draw_with(key, shape, width, reach, cuts, heavy, kind=jnp.bfloat16):
    values = width * jax.random.normal(key, shape, jnp.float32)
    if cuts:
        values = values * steps_of(key, shape, cuts, -0.22, 0.18)
    return jnp.clip(strengthened(values, jax.random.fold_in(key, 3), *heavy), -reach, reach).astype(kind)


def setup_inputs(seed: int = 0) -> dict:
    keys = jax.random.split(jax.random.key(seed), 18)
    return {
        "layer_input": bell_draw_with(keys[0], (ROWS, LEN, D), 1.0, 6.0, ((0, 2), (1, 4)), (1, 2, 4, 2.0)),
        "lengths": draw_lengths(jax.random.fold_in(keys[17], 71), 0),
        "cotangent": noise(keys[2], (ROWS, LEN, D), 1.0, 6.0, ((0, 2), (1, 16))),
        "ln1_gain": jnp.clip(1.0 + 0.1 * jax.random.normal(keys[3], (D,), jnp.float32), 0.5, 1.5).astype(jnp.bfloat16),
        "ln1_bias": noise(keys[4], (D,), 0.5, 3.0),
        "w_query": noise(keys[5], (D, H * HD), D ** -0.5, 0.125, ((1, 4),)),
        "b_query": noise(keys[6], (H * HD,), 0.5, 3.0, ((0, 4),)),
        "w_kv": noise(keys[7], (D, 2 * HD), D ** -0.5, 0.125),
        "b_value": noise(keys[8], (HD,), 0.5, 3.0),
        "w_out": noise(keys[9], (H * HD, D), (H * HD // 16) ** -0.5, 0.5, ((0, 4),)),
        "b_out": noise(keys[10], (D,), 0.5, 3.0),
        "ln2_gain": jnp.clip(1.0 + 0.1 * jax.random.normal(keys[11], (D,), jnp.float32), 0.5, 1.5).astype(jnp.bfloat16),
        "ln2_bias": noise(keys[12], (D,), 0.5, 3.0),
        "w_up": noise(keys[13], (D, FF), D ** -0.5, 0.125, ((1, 4),)),
        "b_up": noise(keys[14], (FF,), 0.5, 3.0, ((0, 4),)),
        "w_down": noise(keys[15], (FF, D), FF ** -0.5, 0.0625, ((0, 4),)),
        "b_down": noise(keys[16], (D,), 0.5, 3.0),
    }


NORM_EPS = 1e-05

@jax.custom_vjp
def low(v):
    return lax.optimization_barrier(v.astype(jnp.bfloat16)).astype(jnp.float32)

@jax.custom_vjp
def low_back(v):
    return v

def low_keep(v):
    return (low(v), None)

def low_pass(kept, grad):
    return (grad,)

def back_keep(v):
    return (v, None)

def back_low(kept, grad):
    return (low(grad),)
low.defvjp(low_keep, low_pass)
low_back.defvjp(back_keep, back_low)

def layer_norm(values_in, norm_gain, norm_bias):
    row_mean = lax.optimization_barrier(jnp.mean(values_in, -1, keepdims=True))
    centered = values_in - row_mean
    variance = lax.optimization_barrier(jnp.mean(centered * centered, -1, keepdims=True))
    return centered * lax.rsqrt(variance + NORM_EPS) * norm_gain + norm_bias

def matmul(left_in, right_in):
    return jnp.dot(left_in, right_in, precision=lax.Precision.HIGHEST)

def forward_row(params_in, row_in, length):
    ln1_gain, ln1_bias, w_query, b_query, w_kv, b_value, w_out, b_out, ln2_gain, ln2_bias, w_up, b_up, w_down, b_down = params_in
    q_scale = 1.0 / math.sqrt(HD)
    positions = jnp.arange(LEN, dtype=jnp.int32)
    is_valid = (positions < length).astype(jnp.float32)
    allowed_keys = (positions[None, :] <= positions[:, None]) & (positions[None, :] < length)
    normed_one = low(layer_norm(row_in, ln1_gain, ln1_bias))
    queries = low(low_back((matmul(normed_one, w_query) + b_query) * q_scale)).reshape(LEN, H, HD)
    kv_bias = jnp.concatenate([jnp.zeros((HD,), jnp.float32), b_value])
    kv_pair = low(low_back(matmul(normed_one, w_kv) + kv_bias))
    key_rows = kv_pair[:, :HD]
    value_rows = kv_pair[:, HD:]
    scores = low_back(jnp.einsum('ihd,jd->hij', queries, key_rows, precision=lax.Precision.HIGHEST))
    scores = jnp.where(allowed_keys[None], scores, -1e+30)
    row_max = lax.optimization_barrier(jnp.max(scores, -1, keepdims=True))
    exp_scores = jnp.exp(scores - row_max)
    soft_probs = exp_scores / lax.optimization_barrier(jnp.sum(exp_scores, -1, keepdims=True))
    mixed_heads = jnp.einsum('hij,jd->ihd', low(soft_probs), value_rows, precision=lax.Precision.HIGHEST)
    mixed_heads = low(low_back(mixed_heads.reshape(LEN, H * HD)))
    residual = row_in + low_back(matmul(mixed_heads, w_out) + b_out)
    normed_two = low(layer_norm(residual, ln2_gain, ln2_bias))
    pre_act = low_back(matmul(normed_two, w_up) + b_up)
    activated = low(jax.nn.gelu(pre_act, approximate=True))
    branch = low_back(matmul(activated, w_down) + b_down)
    return is_valid[:, None] * (residual + branch)

def reference(layer_input, lengths, cotangent, ln1_gain, ln1_bias, w_query, b_query, w_kv, b_value, w_out, b_out, ln2_gain, ln2_bias, w_up, b_up, w_down, b_down):
    params_in = tuple((item.astype(jnp.float32) for item in (ln1_gain, ln1_bias, w_query, b_query, w_kv, b_value, w_out, b_out, ln2_gain, ln2_bias, w_up, b_up, w_down, b_down)))

    def row_step(carried, row_data):
        row_in, length, row_cot = row_data
        row_out, pull_back = jax.vjp(lambda p_in, r_in: forward_row(p_in, r_in, length), params_in, row_in)
        grad_params, grad_row = pull_back(row_cot)
        carried = jax.tree.map(lambda left_in, right_in: left_in + right_in, carried, grad_params)
        return (carried, (row_out.astype(jnp.bfloat16), grad_row))
    start_grads = jax.tree.map(jnp.zeros_like, params_in)
    totals, (layer_output, input_grad) = lax.scan(row_step, start_grads, (layer_input.astype(jnp.float32), lengths, cotangent.astype(jnp.float32)))
    d_ln1_gain, d_ln1_bias, d_w_query, d_b_query, d_w_kv, d_b_value, d_w_out, d_b_out, d_ln2_gain, d_ln2_bias, d_w_up, d_b_up, d_w_down, d_b_down = totals
    small_grads = jnp.stack([d_ln1_gain, d_ln1_bias, d_ln2_gain, d_ln2_bias, d_b_out, d_b_down])
    return (layer_output, input_grad, d_w_query, d_b_query.reshape(H, HD), d_w_kv, d_b_value, d_w_out, d_w_up, d_b_up.reshape(FF // 128, 128), d_w_down, small_grads)
```

```python
import math

import jax
import jax.numpy as jnp
from jax import lax
from jax.sharding import PartitionSpec as P

NORM_EPS = 1e-05
BF16 = jnp.bfloat16
F32 = jnp.float32


def normalize(values_in):
    row_mean = jnp.mean(values_in, -1, keepdims=True)
    centered = values_in - row_mean
    variance = jnp.mean(centered * centered, -1, keepdims=True)
    inv_std = lax.rsqrt(variance + NORM_EPS)
    return (centered * inv_std, inv_std)


def norm_back(grad_in, normed, inv_std, norm_gain):
    scaled = grad_in * norm_gain
    mean_scaled = jnp.mean(scaled, -1, keepdims=True)
    mean_mixed = jnp.mean(scaled * normed, -1, keepdims=True)
    return inv_std * (scaled - mean_scaled - normed * mean_mixed)


def across_rows(left_in, right_in):
    return lax.dot_general(left_in, right_in, (((0,), (0,)), ((), ())), preferred_element_type=F32)


def times_transposed(left_in, right_in):
    return lax.dot_general(left_in, right_in, (((1,), (1,)), ((), ())), preferred_element_type=F32)


def dp_exchange(part_for):
    n_dp = lax.axis_size("dp")
    me = lax.axis_index("dp")
    arrived = []
    for k in range(1, n_dp):
        target = lax.rem(me + k, n_dp)
        pairs = [(i, (i + k) % n_dp) for i in range(n_dp)]
        arrived.append(lax.ppermute(part_for(target).astype(BF16), "dp", pairs))
    total = part_for(me)
    for piece in arrived:
        total = total + piece.astype(F32)
    return total


def two_stage(part_for, dim):
    total = dp_exchange(part_for)
    return lax.psum_scatter(total.astype(BF16), "seq", scatter_dimension=dim, tiled=True).astype(F32)


def shards(
    layer_input,
    lengths,
    cotangent,
    ln1_gain,
    ln1_bias,
    w_query,
    b_query,
    w_kv,
    b_value,
    w_out,
    b_out,
    ln2_gain,
    ln2_bias,
    w_up,
    b_up,
    w_down,
    b_down,
):
    n_rows, seq_len, model_width = layer_input.shape
    n_tensor = lax.axis_size("tensor")
    n_dp = lax.axis_size("dp")
    n_seq = lax.axis_size("seq")
    share_len = seq_len // n_tensor
    tensor_index = lax.axis_index("tensor")
    seq_index = lax.axis_index("seq")
    full_len = seq_len * n_seq
    head_size = w_kv.shape[1] // 2
    num_heads = w_query.shape[1] // head_size
    q_scale = 1.0 / math.sqrt(head_size)
    n_tok = n_rows * seq_len
    n_own = n_rows * share_len

    def own_rows(values_in):
        return lax.dynamic_slice_in_dim(values_in, tensor_index * share_len, share_len, 1)

    def gather_own(values_in):
        return lax.all_gather(values_in, "tensor", axis=1, tiled=True)

    def scatter_own(values_in):
        return lax.psum_scatter(
            values_in.astype(BF16).reshape(n_rows, seq_len, model_width), "tensor", scatter_dimension=1, tiled=True
        ).astype(F32)

    positions = seq_index * seq_len + jnp.arange(seq_len, dtype=jnp.int32)
    key_places = jnp.arange(full_len, dtype=jnp.int32)
    is_valid = (positions[None, :] < lengths[:, None]).astype(F32)
    allowed_keys = (key_places[None, None, :] <= positions[None, :, None]) & (
        key_places[None, None, :] < lengths[:, None, None]
    )
    valid_own = own_rows(is_valid)
    x_float = layer_input.astype(F32)
    normed_x1, inv_one = normalize(x_float)
    normed_one = (normed_x1 * ln1_gain + ln1_bias).astype(BF16)
    flat_one = normed_one.reshape(n_tok, model_width)
    kv_bias = jnp.concatenate([jnp.zeros((head_size,), F32), b_value.astype(F32)])
    kv_local = (jnp.dot(flat_one, w_kv, preferred_element_type=F32) + kv_bias).astype(BF16)
    kv_local = kv_local.reshape(n_rows, seq_len, 2 * head_size)
    kv_all = lax.all_gather(kv_local, "seq", axis=1, tiled=True)
    queries = ((jnp.dot(flat_one, w_query, preferred_element_type=F32) + b_query) * q_scale).astype(BF16)
    queries = queries.reshape(n_rows, seq_len, num_heads, head_size)
    key_rows = kv_all[..., :head_size]
    value_rows = kv_all[..., head_size:]
    grad_y_own = cotangent.astype(F32) * valid_own[..., None]
    grad_y_low = gather_own(grad_y_own.astype(BF16)).reshape(n_tok, model_width)

    def scores_of(query_rows):
        raw_scores = jnp.einsum("rshd,rld->rhsl", query_rows, key_rows, preferred_element_type=F32)
        return jnp.where(allowed_keys[:, None], raw_scores, -1e30)

    scores = scores_of(queries)
    row_max = jnp.max(scores, -1, keepdims=True)
    exp_scores = jnp.exp(scores - row_max)
    exp_total = jnp.sum(exp_scores, -1, keepdims=True)
    soft_probs = exp_scores / exp_total
    log_total = row_max + jnp.log(exp_total)
    mixed_heads = jnp.einsum(
        "rhsl,rld->rshd", soft_probs.astype(BF16), value_rows, preferred_element_type=F32
    ).astype(BF16)
    mixed_heads = mixed_heads.reshape(n_tok, num_heads * head_size)
    attn_own = scatter_own(jnp.dot(mixed_heads, w_out, preferred_element_type=F32))
    x_own = own_rows(x_float)
    resid_own = x_own + (attn_own + b_out)
    normed_x2, inv_two = normalize(resid_own)
    normed_two = (normed_x2 * ln2_gain + ln2_bias).astype(BF16)
    flat_two = gather_own(normed_two).reshape(n_tok, model_width)
    pre_act = jnp.dot(flat_two, w_up, preferred_element_type=F32) + b_up
    activated, gelu_pull = jax.vjp(lambda inner_in: jax.nn.gelu(inner_in, approximate=True), pre_act)
    act_low = activated.astype(BF16)
    grad_act = times_transposed(grad_y_low, w_down)
    grad_pre = gelu_pull(grad_act)[0].astype(BF16)

    half_width = model_width // n_dp

    def columns(values_in, d):
        return lax.dynamic_slice_in_dim(values_in, d * half_width, half_width, 1)

    grad_n2 = scatter_own(times_transposed(grad_pre, w_up))
    g_w_down = two_stage(lambda d: across_rows(act_low, columns(grad_y_low, d)), 1)
    g_w_up = two_stage(lambda d: across_rows(columns(flat_two, d), grad_pre), 0)
    g_b_up = jnp.sum(grad_pre.astype(F32), axis=0)
    mlp_own = scatter_own(jnp.dot(act_low, w_down, preferred_element_type=F32)) + b_down
    y_own = (valid_own[..., None] * (resid_own + mlp_own)).astype(BF16)
    grad_resid = grad_y_own + norm_back(grad_n2, normed_x2, inv_two, ln2_gain)
    grad_resid_low = grad_resid.astype(BF16)
    flat_resid = gather_own(grad_resid_low).reshape(n_tok, model_width)
    g_ln2_gain = jnp.sum(grad_n2 * normed_x2, axis=(0, 1))
    g_ln2_bias = jnp.sum(grad_n2, axis=(0, 1))
    g_b_out = jnp.sum(grad_resid_low.astype(F32), axis=(0, 1))
    g_b_down = jnp.sum(grad_y_own, axis=(0, 1))
    g_w_out = two_stage(lambda d: across_rows(mixed_heads, columns(flat_resid, d)), 1)
    grad_mixed = times_transposed(flat_resid, w_out).astype(BF16)
    grad_mixed = grad_mixed.reshape(n_rows, seq_len, num_heads, head_size)
    again_probs = jnp.exp(scores_of(queries) - log_total)
    grad_probs = jnp.einsum("rshd,rld->rhsl", grad_mixed, value_rows, preferred_element_type=F32)
    inner_sum = jnp.sum(again_probs * grad_probs, -1, keepdims=True)
    grad_scores = (again_probs * (grad_probs - inner_sum)).astype(BF16)
    grad_query = jnp.einsum("rhsl,rld->rshd", grad_scores, key_rows, preferred_element_type=F32).astype(BF16)
    grad_keys = jnp.einsum("rhsl,rshd->rld", grad_scores, queries, preferred_element_type=F32)
    grad_values = jnp.einsum(
        "rhsl,rshd->rld", again_probs.astype(BF16), grad_mixed, preferred_element_type=F32
    )
    grad_kv = jnp.concatenate([grad_keys, grad_values], -1)
    grad_kv_own = lax.psum_scatter(
        grad_kv.astype(BF16), "seq", scatter_dimension=1, tiled=True
    )
    grad_kv_own = lax.psum_scatter(grad_kv_own, "tensor", scatter_dimension=1, tiled=True)
    flat_query = grad_query.reshape(n_tok, num_heads * head_size)
    g_b_query = jnp.sum(flat_query.astype(F32), axis=0) * q_scale
    grad_n1 = scatter_own(times_transposed(flat_query, w_query) * q_scale)
    g_w_query = two_stage(lambda d: across_rows(columns(flat_one, d), flat_query) * q_scale, 0)
    flat_kv = grad_kv_own.reshape(n_own, 2 * head_size)
    grad_n1 = grad_n1 + times_transposed(flat_kv, w_kv).reshape(n_rows, share_len, model_width)
    one_own = own_rows(normed_one).reshape(n_own, model_width)
    g_w_kv = across_rows(one_own, flat_kv)
    g_b_value = jnp.sum(flat_kv[:, head_size:].astype(F32), axis=0)
    normed_x1_own = own_rows(normed_x1)
    x_grad_own = grad_resid + norm_back(grad_n1, normed_x1_own, own_rows(inv_one), ln1_gain)
    g_ln1_gain = jnp.sum(grad_n1 * normed_x1_own, axis=(0, 1))
    g_ln1_bias = jnp.sum(grad_n1, axis=(0, 1))
    owners = n_dp * n_seq
    small = jnp.stack([g_ln1_gain, g_ln1_bias, g_ln2_gain, g_ln2_bias, g_b_out, g_b_down])
    kv_piece = g_w_kv.reshape(owners, n_tensor, -1)
    small_width = model_width // (owners * n_tensor)
    small_piece = jnp.moveaxis(small.reshape(6, owners, n_tensor, small_width), 0, 2).reshape(owners, n_tensor, -1)
    value_piece = g_b_value.reshape(owners, n_tensor, -1)
    packed = jnp.concatenate([kv_piece, small_piece, value_piece], -1)
    packed = lax.psum_scatter(packed.astype(BF16), "tensor", scatter_dimension=1, tiled=True).astype(F32)[:, 0]
    query_table = jnp.moveaxis(g_b_query.reshape(num_heads, owners, -1), 1, 0).reshape(owners, -1)
    up_table = jnp.moveaxis(g_b_up.reshape(-1, owners, 128 // owners), 1, 0).reshape(owners, -1)
    packed = jnp.concatenate([packed, query_table, up_table], -1)
    packed = lax.psum_scatter(packed.astype(BF16), ("dp", "seq"), scatter_dimension=0, tiled=True).astype(F32)[0]
    sizes = [kv_piece.shape[-1], small_piece.shape[-1], value_piece.shape[-1], query_table.shape[-1], up_table.shape[-1]]
    ends = [sum(sizes[: i + 1]) for i in range(len(sizes))]
    kv_out, small_out, value_out, query_out, up_out = [packed[e - s : e] for s, e in zip(sizes, ends)]
    return (
        y_own,
        x_grad_own,
        g_w_query,
        query_out.reshape(num_heads, -1),
        kv_out.reshape(-1, 2 * head_size),
        value_out,
        g_w_out,
        g_w_up,
        up_out.reshape(-1, 128 // owners),
        g_w_down,
        small_out.reshape(6, -1),
    )


def solution(mesh):
    placed = (
        P("dp", "seq", None),
        P("dp"),
        P("dp", ("seq", "tensor"), None),
        P(),
        P(),
        P(None, "tensor"),
        P("tensor"),
        P(),
        P(),
        P("tensor", None),
        P(),
        P(),
        P(),
        P(None, "tensor"),
        P("tensor"),
        P("tensor", None),
        P(),
    )
    return jax.shard_map(
        shards,
        mesh=mesh,
        in_specs=placed,
        out_specs=(
            P("dp", ("seq", "tensor"), None),
            P("dp", ("seq", "tensor"), None),
            P(("dp", "seq"), "tensor"),
            P("tensor", ("dp", "seq")),
            P(("dp", "seq", "tensor"), None),
            P(("dp", "seq", "tensor")),
            P("tensor", ("dp", "seq")),
            P(("dp", "seq"), "tensor"),
            P("tensor", ("dp", "seq")),
            P("tensor", ("dp", "seq")),
            P(None, ("dp", "seq", "tensor")),
        ),
        check_vma=False,
    )
```

```python
import functools
import math

import jax
import jax.numpy as jnp
from jax import lax
from jax.experimental import pallas as pl
from jax.experimental.pallas import tpu as pltpu
from jax.sharding import PartitionSpec as P

NORM_EPS = 1e-05
BF16 = jnp.bfloat16
F32 = jnp.float32
MESH = pl.DeviceIdType.MESH


def normalize(values_in):
    row_mean = jnp.mean(values_in, -1, keepdims=True)
    centered = values_in - row_mean
    variance = jnp.mean(centered * centered, -1, keepdims=True)
    inv_std = lax.rsqrt(variance + NORM_EPS)
    return (centered * inv_std, inv_std)


def norm_back(grad_in, normed, inv_std, norm_gain):
    scaled = grad_in * norm_gain
    mean_scaled = jnp.mean(scaled, -1, keepdims=True)
    mean_mixed = jnp.mean(scaled * normed, -1, keepdims=True)
    return inv_std * (scaled - mean_scaled - normed * mean_mixed)


def across_rows(left_in, right_in):
    return lax.dot_general(left_in, right_in, (((0,), (0,)), ((), ())), preferred_element_type=F32)


def times_transposed(left_in, right_in):
    return lax.dot_general(left_in, right_in, (((1,), (1,)), ((), ())), preferred_element_type=F32)


def dp_exchange(part_for):
    n_dp = lax.axis_size("dp")
    me = lax.axis_index("dp")
    arrived = []
    for k in range(1, n_dp):
        target = lax.rem(me + k, n_dp)
        pairs = [(i, (i + k) % n_dp) for i in range(n_dp)]
        arrived.append(lax.ppermute(part_for(target).astype(BF16), "dp", pairs))
    total = part_for(me)
    for piece in arrived:
        total = total + piece.astype(F32)
    return total


def two_stage(part_for, dim):
    total = dp_exchange(part_for)
    return lax.psum_scatter(total.astype(BF16), "seq", scatter_dimension=dim, tiled=True).astype(F32)


def from_all_dp(values_in):
    n_dp = lax.axis_size("dp")
    pieces = [values_in]
    for k in range(1, n_dp):
        pieces.append(lax.ppermute(values_in, "dp", [(i, (i + k) % n_dp) for i in range(n_dp)]))
    return pieces


def columns_from_all_dp(values_in):
    n_dp = lax.axis_size("dp")
    me = lax.axis_index("dp")
    width = values_in.shape[1] // n_dp
    pieces = [lax.dynamic_slice_in_dim(values_in, me * width, width, 1)]
    for k in range(1, n_dp):
        sent = lax.dynamic_slice_in_dim(values_in, lax.rem(me + k, n_dp) * width, width, 1)
        pieces.append(lax.ppermute(sent, "dp", [(i, (i + k) % n_dp) for i in range(n_dp)]))
    return pieces


def tensor_partners():
    here = lax.axis_index("tensor")
    core = lax.rem(here, 2)
    chip = here // 2
    return here, chip, core, 2 * chip + 1 - core, 2 * (1 - chip) + core


def greet(*targets):
    barrier = pltpu.get_barrier_semaphore()
    for target in targets:
        pl.semaphore_signal(barrier, inc=1, device_id={"tensor": target}, device_id_type=MESH)
    pl.semaphore_wait(barrier, len(targets))


def send(source, landing, send_sem, recv_sem, target):
    return pltpu.make_async_remote_copy(
        src_ref=source,
        dst_ref=landing,
        send_sem=send_sem,
        recv_sem=recv_sem,
        device_id={"tensor": target},
        device_id_type=MESH,
    )


def reduce_kernel(
    transposed, a_ref, w_ref, o_ref, w_here, part, core_out, core_in, over_out, over_in, w_sem, cs, cr, xs, xr
):
    n_blocks, width = core_out.shape[0], core_out.shape[-1]
    share = o_ref.shape[0]
    _, chip, core, partner, across = tensor_partners()

    def load(n):
        where = pl.ds(n * width, width)
        block = w_ref.at[where, :] if transposed else w_ref.at[:, where]
        return pltpu.make_async_copy(block, w_here.at[n], w_sem.at[n])

    def to_partner(n):
        return send(core_out.at[n], core_in.at[n], cs.at[n], cr.at[n], partner)

    def to_across(n):
        return send(over_out.at[n], over_in.at[n], xs.at[n], xr.at[n], across)

    for n in range(n_blocks):
        load(n).start()
    greet(partner, across)

    def multiply(n):
        load(n).wait()
        slot = lax.rem(n, 2)
        dims = (((1,), (1,)), ((), ())) if transposed else (((1,), (0,)), ((), ()))
        product = lax.dot_general(a_ref[...], w_here[n], dims, preferred_element_type=F32)
        part[slot] = product.reshape(4, share, width)
        core_out[n, 0] = part[slot, 1 - core].astype(BF16)
        core_out[n, 1] = part[slot, 3 - core].astype(BF16)
        to_partner(n).start()

    def pass_on(n):
        slot = lax.rem(n, 2)
        to_partner(n).wait_recv()
        over_out[n] = (part[slot, 2 * (1 - chip) + core] + core_in[n, 1 - chip].astype(F32)).astype(BF16)
        to_across(n).start()
        columns = pl.ds(pl.multiple_of(n * width, width), width)
        o_ref[:, columns] = part[slot, 2 * chip + core] + core_in[n, chip].astype(F32)

    def step(n, carry):
        multiply(n)

        @pl.when(n > 0)
        def _():
            pass_on(n - 1)

        return carry

    lax.fori_loop(0, n_blocks, step, 0)
    pass_on(n_blocks - 1)

    def finish(n, carry):
        to_across(n).wait_recv()
        columns = pl.ds(pl.multiple_of(n * width, width), width)
        o_ref[:, columns] += over_in[n].astype(F32)
        to_across(n).wait_send()
        to_partner(n).wait_send()
        return carry

    lax.fori_loop(0, n_blocks, finish, 0)


def product_to_owners(name, number, a, w, transposed):
    tokens, depth = a.shape
    model_width = w.shape[0] if transposed else w.shape[1]
    share = tokens // 4
    width = model_width // 4
    n_blocks = 4
    w_block = (n_blocks, width, depth) if transposed else (n_blocks, depth, width)
    dma = pltpu.SemaphoreType.DMA((n_blocks,))
    return pl.pallas_call(
        functools.partial(reduce_kernel, transposed),
        out_shape=jax.ShapeDtypeStruct((share, model_width), F32),
        in_specs=[pl.BlockSpec(memory_space=pltpu.VMEM), pl.BlockSpec(memory_space=pl.ANY)],
        out_specs=pl.BlockSpec(memory_space=pltpu.VMEM),
        scratch_shapes=[
            pltpu.VMEM(w_block, BF16),
            pltpu.VMEM((2, 4, share, width), F32),
            pltpu.VMEM((n_blocks, 2, share, width), BF16),
            pltpu.VMEM((n_blocks, 2, share, width), BF16),
            pltpu.VMEM((n_blocks, share, width), BF16),
            pltpu.VMEM((n_blocks, share, width), BF16),
            dma,
            dma,
            dma,
            dma,
            dma,
        ],
        compiler_params=pltpu.CompilerParams(
            collective_id=number, has_side_effects=True, vmem_limit_bytes=40 * 1024 * 1024
        ),
        cost_estimate=estimate(25),
        name=name,
    )(a, w)


def gather_kernel(own_ref, o_ref, cs, cr, xs, xr, fs, fr):
    n_chunks = cs.shape[0]
    share = own_ref.shape[0]
    rows = share // n_chunks
    here, _, _, partner, across = tensor_partners()

    def copy(source, owner, n, sems, target):
        where = pl.ds(n * rows, rows)
        return send(source.at[where], o_ref.at[owner, where], sems[0].at[n], sems[1].at[n], target)

    greet(partner, across)
    for n in range(n_chunks):
        copy(own_ref, here, n, (xs, xr), across).start()
    for n in range(n_chunks):
        copy(own_ref, here, n, (cs, cr), partner).start()
    o_ref[here] = own_ref[...]
    for n in range(n_chunks):
        copy(own_ref, here, n, (xs, xr), across).wait_recv()
        copy(o_ref.at[across], across, n, (fs, fr), partner).start()
    for n in range(n_chunks):
        copy(own_ref, here, n, (xs, xr), across).wait_send()
        copy(own_ref, here, n, (cs, cr), partner).wait()
        copy(o_ref.at[across], across, n, (fs, fr), partner).wait()


def gather_shares(name, number, own):
    share, width = own.shape
    dma = pltpu.SemaphoreType.DMA((4,))
    return pl.pallas_call(
        gather_kernel,
        out_shape=jax.ShapeDtypeStruct((4, share, width), own.dtype),
        in_specs=[pl.BlockSpec(memory_space=pltpu.VMEM)],
        out_specs=pl.BlockSpec(memory_space=pltpu.VMEM),
        scratch_shapes=[dma] * 6,
        compiler_params=pltpu.CompilerParams(
            collective_id=number, has_side_effects=True, vmem_limit_bytes=16 * 1024 * 1024
        ),
        cost_estimate=estimate(20),
        name=name,
    )(own).reshape(4 * share, width)


def remote(source, landing, send_sem, recv_sem, target):
    return pltpu.make_async_remote_copy(
        src_ref=source,
        dst_ref=landing,
        send_sem=send_sem,
        recv_sem=recv_sem,
        device_id=target,
        device_id_type=MESH,
    )


def greet_all(targets):
    barrier = pltpu.get_barrier_semaphore()
    for target in targets:
        pl.semaphore_signal(barrier, inc=1, device_id=target, device_id_type=MESH)
    pl.semaphore_wait(barrier, len(targets))


def others_along(axis):
    size = lax.axis_size(axis)
    me = lax.axis_index(axis)
    return me, [lax.rem(me + k, size) for k in range(1, size)]


def small_kernel(in_ref, o_ref, core_in, over_out, over_in, dp_out, dp_in, seq_out, seq_in, cs, cr, xs, xr, ys, yr, zs, zr):
    _, chip, core, partner, across = tensor_partners()
    dp_me, dp_others = others_along("dp")
    seq_me, seq_others = others_along("seq")
    greet_all(
        [{"tensor": partner}, {"tensor": across}]
        + [{"dp": other} for other in dp_others]
        + [{"seq": other} for other in seq_others]
    )

    def to_partner(j):
        return remote(in_ref.at[j, 1 - core], core_in.at[j], cs.at[j], cr.at[j], {"tensor": partner})

    to_partner(0).start()
    to_partner(1).start()
    to_partner(0).wait()
    to_partner(1).wait()
    over_out[...] = in_ref[1 - chip, core] + core_in[1 - chip]
    to_across = remote(over_out, over_in, xs.at[0], xr.at[0], {"tensor": across})
    to_across.start()
    to_across.wait()
    dp_out[...] = in_ref[chip, core] + core_in[chip] + over_in[...]

    def fold(outgoing, incoming, send_sems, recv_sems, axis, me, others):
        def copy(target):
            return remote(outgoing.at[target], incoming.at[me], send_sems.at[target], recv_sems.at[me], {axis: target})

        for other in others:
            copy(other).start()
        total = outgoing[me]
        for other in others:
            remote(
                outgoing.at[other], incoming.at[other], send_sems.at[other], recv_sems.at[other], {axis: other}
            ).wait_recv()
            total = total + incoming[other]
        for other in others:
            copy(other).wait_send()
        return total

    seq_out[...] = fold(dp_out, dp_in, ys, yr, "dp", dp_me, dp_others)
    o_ref[...] = fold(seq_out, seq_in, zs, zr, "seq", seq_me, seq_others)


def sum_small(number, packed):
    n_dp, n_seq, rows, lanes = packed.shape[2:]
    dma = pltpu.SemaphoreType.DMA
    return pl.pallas_call(
        small_kernel,
        out_shape=jax.ShapeDtypeStruct((rows, lanes), F32),
        in_specs=[pl.BlockSpec(memory_space=pltpu.VMEM)],
        out_specs=pl.BlockSpec(memory_space=pltpu.VMEM),
        scratch_shapes=[
            pltpu.VMEM((2, n_dp, n_seq, rows, lanes), F32),
            pltpu.VMEM((n_dp, n_seq, rows, lanes), F32),
            pltpu.VMEM((n_dp, n_seq, rows, lanes), F32),
            pltpu.VMEM((n_dp, n_seq, rows, lanes), F32),
            pltpu.VMEM((n_dp, n_seq, rows, lanes), F32),
            pltpu.VMEM((n_seq, rows, lanes), F32),
            pltpu.VMEM((n_seq, rows, lanes), F32),
            dma((2,)),
            dma((2,)),
            dma((1,)),
            dma((1,)),
            dma((n_dp,)),
            dma((n_dp,)),
            dma((n_seq,)),
            dma((n_seq,)),
        ],
        compiler_params=pltpu.CompilerParams(collective_id=number, has_side_effects=True),
        cost_estimate=estimate(12),
        name="sum_small",
    )(packed)


def kv_kernel(
    g_ref, o_ref, core_in, over_out, over_in, seq_out, seq_in, own, cs, cr, xs, xr, zs, zr, gs, gr
):
    here, chip, core, partner, across = tensor_partners()
    seq_me, seq_others = others_along("seq")
    greet_all(
        [{"tensor": partner}, {"tensor": across}] + [{"seq": other} for other in seq_others]
    )

    def to_partner(j):
        return remote(g_ref.at[2 * j + 1 - core], core_in.at[j], cs.at[j], cr.at[j], {"tensor": partner})

    to_partner(1 - chip).start()
    to_partner(chip).start()
    to_partner(1 - chip).wait()
    over_out[...] = (g_ref[2 * (1 - chip) + core].astype(F32) + core_in[1 - chip].astype(F32)).astype(BF16)
    to_across = remote(over_out, over_in, xs.at[0], xr.at[0], {"tensor": across})
    to_across.start()
    to_partner(chip).wait()
    to_across.wait()
    seq_out[...] = (
        g_ref[2 * chip + core].astype(F32) + core_in[chip].astype(F32) + over_in[...].astype(F32)
    ).astype(BF16)

    def to_seq(target):
        return remote(seq_out.at[target], seq_in.at[seq_me], zs.at[target], zr.at[seq_me], {"seq": target})

    for other in seq_others:
        to_seq(other).start()
    total = seq_out[seq_me].astype(F32)
    for other in seq_others:
        remote(seq_out.at[other], seq_in.at[other], zs.at[other], zr.at[other], {"seq": other}).wait_recv()
        total = total + seq_in[other].astype(F32)
    own[...] = total.astype(BF16)
    o_ref[here] = own[...]
    x_copy = remote(own, o_ref.at[here], gs.at[0], gr.at[0], {"tensor": across})
    c_copy = remote(own, o_ref.at[here], gs.at[1], gr.at[1], {"tensor": partner})
    x_copy.start()
    c_copy.start()
    x_copy.wait_recv()
    f_copy = remote(o_ref.at[across], o_ref.at[across], gs.at[2], gr.at[2], {"tensor": partner})
    f_copy.start()
    x_copy.wait_send()
    c_copy.wait()
    f_copy.wait()
    for other in seq_others:
        to_seq(other).wait_send()


def sum_grad_kv(number, parts):
    _, n_seq, share, width = parts.shape
    dma = pltpu.SemaphoreType.DMA
    return pl.pallas_call(
        kv_kernel,
        out_shape=jax.ShapeDtypeStruct((4, share, width), BF16),
        in_specs=[pl.BlockSpec(memory_space=pltpu.VMEM)],
        out_specs=pl.BlockSpec(memory_space=pltpu.VMEM),
        scratch_shapes=[
            pltpu.VMEM((2, n_seq, share, width), BF16),
            pltpu.VMEM((n_seq, share, width), BF16),
            pltpu.VMEM((n_seq, share, width), BF16),
            pltpu.VMEM((n_seq, share, width), BF16),
            pltpu.VMEM((n_seq, share, width), BF16),
            pltpu.VMEM((share, width), BF16),
            dma((2,)),
            dma((2,)),
            dma((1,)),
            dma((1,)),
            dma((n_seq,)),
            dma((n_seq,)),
            dma((3,)),
            dma((3,)),
        ],
        compiler_params=pltpu.CompilerParams(collective_id=number, has_side_effects=True),
        cost_estimate=estimate(30),
        name="sum_grad_kv",
    )(parts).reshape(4 * share, width)


def estimate(microseconds):
    return pl.CostEstimate(flops=int(microseconds * 1e9), bytes_accessed=0, transcendentals=0)


def together(values, *earlier):
    return lax.optimization_barrier(tuple(values) + earlier)[: len(values)]


def after(value, *earlier):
    return lax.optimization_barrier((value,) + earlier)[0]


def shards(
    layer_input,
    lengths,
    cotangent,
    ln1_gain,
    ln1_bias,
    w_query,
    b_query,
    w_kv,
    b_value,
    w_out,
    b_out,
    ln2_gain,
    ln2_bias,
    w_up,
    b_up,
    w_down,
    b_down,
):
    n_rows, seq_len, model_width = layer_input.shape
    n_tensor = lax.axis_size("tensor")
    n_dp = lax.axis_size("dp")
    n_seq = lax.axis_size("seq")
    share_len = seq_len // n_tensor
    tensor_index = lax.axis_index("tensor")
    seq_index = lax.axis_index("seq")
    full_len = seq_len * n_seq
    head_size = w_kv.shape[1] // 2
    num_heads = w_query.shape[1] // head_size
    q_scale = 1.0 / math.sqrt(head_size)
    n_tok = n_rows * seq_len
    n_own = n_rows * share_len

    def by_share(values_in):
        return jnp.moveaxis(values_in.reshape((n_rows, n_tensor, share_len) + values_in.shape[2:]), 1, 0)

    def by_row(values_in):
        return jnp.moveaxis(
            values_in.reshape((n_tensor, n_rows, share_len) + values_in.shape[1:]), 0, 1
        ).reshape((n_rows, seq_len) + values_in.shape[1:])

    def own_share(values_in):
        return lax.dynamic_index_in_dim(values_in.reshape((n_tensor, n_own) + values_in.shape[1:]), tensor_index, 0, False)

    positions = seq_index * seq_len + jnp.arange(seq_len, dtype=jnp.int32)
    key_places = jnp.arange(full_len, dtype=jnp.int32)
    is_valid = (positions[None, :] < lengths[:, None]).astype(F32)
    allowed_keys = (key_places[None, None, :] <= positions[None, :, None]) & (
        key_places[None, None, :] < lengths[:, None, None]
    )
    valid_own = own_share(by_share(is_valid).reshape(n_tok))[:, None]
    grad_y_own = cotangent.reshape(n_own, model_width).astype(F32) * valid_own
    x_float = by_share(layer_input).reshape(n_tok, model_width).astype(F32)
    normed_x1, inv_one = normalize(x_float)
    flat_one = (normed_x1 * ln1_gain + ln1_bias).astype(BF16)
    kv_bias = jnp.concatenate([jnp.zeros((head_size,), F32), b_value.astype(F32)])
    kv_local = (jnp.dot(flat_one, w_kv, preferred_element_type=F32) + kv_bias).astype(BF16)
    kv_all = lax.all_gather(by_row(kv_local), "seq", axis=1, tiled=True)
    queries = ((jnp.dot(flat_one, w_query, preferred_element_type=F32) + b_query) * q_scale).astype(BF16)
    queries = by_row(queries).reshape(n_rows, seq_len, num_heads, head_size)
    key_rows = kv_all[..., :head_size]
    value_rows = kv_all[..., head_size:]
    grad_y_low = gather_shares("gather_grad_y", 0, grad_y_own.astype(BF16))
    grad_y_columns = columns_from_all_dp(grad_y_low)

    def scores_of(query_rows):
        raw_scores = jnp.einsum("rshd,rld->rhsl", query_rows, key_rows, preferred_element_type=F32)
        return jnp.where(allowed_keys[:, None], raw_scores, -1e30)

    scores = scores_of(queries)
    row_max = jnp.max(scores, -1, keepdims=True)
    exp_scores = jnp.exp(scores - row_max)
    exp_total = jnp.sum(exp_scores, -1, keepdims=True)
    soft_probs = exp_scores / exp_total
    log_total = row_max + jnp.log(exp_total)
    mixed_heads = jnp.einsum(
        "rhsl,rld->rshd", soft_probs.astype(BF16), value_rows, preferred_element_type=F32
    ).astype(BF16)
    mixed_heads = by_share(mixed_heads).reshape(n_tok, num_heads * head_size)
    attn_own = product_to_owners("attn_out", 1, mixed_heads, w_out, False)
    x_own = own_share(x_float)
    resid_own = x_own + (attn_own + b_out)
    normed_x2, inv_two = normalize(resid_own)
    normed_two = (normed_x2 * ln2_gain + ln2_bias).astype(BF16)
    flat_two = gather_shares("gather_norm_two", 2, normed_two)
    two_columns = columns_from_all_dp(flat_two)
    pre_act = jnp.dot(flat_two, w_up, preferred_element_type=F32) + b_up
    activated, gelu_pull = jax.vjp(lambda inner_in: jax.nn.gelu(inner_in, approximate=True), pre_act)
    act_low = activated.astype(BF16)
    grad_act = times_transposed(grad_y_low, w_down)
    grad_pre = gelu_pull(grad_act)[0].astype(BF16)
    grad_pre, act_low = lax.optimization_barrier((grad_pre, act_low))

    half_width = model_width // n_dp
    half_hidden = act_low.shape[1] // 2

    def columns(values_in, d):
        return lax.dynamic_slice_in_dim(values_in, d * half_width, half_width, 1)

    def summed_products(lefts, rights, dim):
        total = across_rows(lefts[0], rights[0])
        for left_in, right_in in zip(lefts[1:], rights[1:]):
            total = total + across_rows(left_in, right_in)
        return total.astype(BF16)

    def over_seq(values_in, dim):
        return lax.psum_scatter(values_in, "seq", scatter_dimension=dim, tiled=True)

    act_a = from_all_dp(act_low[:, :half_hidden])
    grad_n2 = product_to_owners("grad_norm_two", 3, grad_pre, w_up, True)
    grad_resid = grad_y_own + norm_back(grad_n2, normed_x2, inv_two, ln2_gain)
    grad_resid_low = grad_resid.astype(BF16)
    act_b = from_all_dp(after(act_low[:, half_hidden:], grad_resid_low))
    act_a = together(act_a, grad_resid_low, *two_columns)
    part_a = summed_products(act_a, grad_y_columns, 1)
    g_w_down_a = over_seq(part_a, 1)
    flat_resid = gather_shares("gather_grad_resid", 4, after(grad_resid_low, part_a))
    pre_a = from_all_dp(after(grad_pre[:, :half_hidden], flat_resid))
    mlp_own = product_to_owners("mlp_out", 5, after(act_low, flat_resid), w_down, False) + b_down
    part_b = summed_products(together(act_b, mlp_own, g_w_down_a), grad_y_columns, 1)
    g_w_down_b = over_seq(part_b, 1)
    pre_b = from_all_dp(after(grad_pre[:, half_hidden:], part_b))
    flat_resid = after(flat_resid, part_b)
    grad_mixed = times_transposed(flat_resid, w_out).astype(BF16)
    grad_mixed = by_row(grad_mixed).reshape(n_rows, seq_len, num_heads, head_size)
    again_probs = jnp.exp(scores_of(queries) - log_total)
    grad_probs = jnp.einsum("rshd,rld->rhsl", grad_mixed, value_rows, preferred_element_type=F32)
    inner_sum = jnp.sum(again_probs * grad_probs, -1, keepdims=True)
    grad_scores = (again_probs * (grad_probs - inner_sum)).astype(BF16)
    grad_query = jnp.einsum("rhsl,rld->rshd", grad_scores, key_rows, preferred_element_type=F32).astype(BF16)
    grad_keys = jnp.einsum("rhsl,rshd->rld", grad_scores, queries, preferred_element_type=F32)
    grad_values = jnp.einsum(
        "rhsl,rshd->rld", again_probs.astype(BF16), grad_mixed, preferred_element_type=F32
    )
    grad_kv = jnp.concatenate([grad_keys, grad_values], -1).astype(BF16)
    flat_query = by_share(grad_query).reshape(n_tok, num_heads * head_size)
    up_a = summed_products(two_columns, together(pre_a, flat_query, grad_kv, g_w_down_b), 0)
    g_w_up_a = over_seq(up_a, 0)
    flat_query, grad_kv, _ = lax.optimization_barrier((flat_query, grad_kv, up_a))
    grad_kv = jnp.transpose(
        grad_kv.reshape(n_rows, n_seq, n_tensor, share_len, 2 * head_size), (2, 1, 0, 3, 4)
    ).reshape(n_tensor, n_seq, n_own, 2 * head_size)
    flat_kv = sum_grad_kv(7, grad_kv)
    kv_columns = lax.dynamic_index_in_dim(
        flat_one.reshape(n_tok, n_dp * n_seq, n_tensor, model_width // (n_dp * n_seq * n_tensor)), tensor_index, 2, False
    )

    def first_part(d):
        query_part = across_rows(columns(flat_one, d), flat_query) * q_scale
        kv_side = lax.dynamic_slice_in_dim(kv_columns, d * n_seq, n_seq, 1).reshape(n_tok, -1)
        kv_part = across_rows(kv_side, flat_kv)
        out_part = across_rows(columns(flat_resid, d), mixed_heads)
        pieces = [p.reshape(n_seq, -1, query_part.shape[1]) for p in (query_part, kv_part, out_part)]
        return jnp.concatenate(pieces, 1)

    last_part = dp_exchange(first_part)
    grad_n1 = product_to_owners("grad_norm_one", 6, after(flat_query, flat_kv), w_query, True) * q_scale
    up_b = summed_products(two_columns, together(pre_b, grad_n1, g_w_up_a), 0)
    g_w_up_b = over_seq(up_b, 0)
    last_part = after(last_part, up_b).astype(BF16)
    last_sum = lax.psum_scatter(last_part, "seq", scatter_dimension=0, tiled=True)[0].astype(F32)
    last_rows = model_width // (n_dp * n_seq)
    g_w_query = last_sum[:last_rows]
    g_w_out = jnp.transpose(last_sum[-last_rows:])
    g_w_kv = last_sum[last_rows:-last_rows].reshape(-1, 2 * head_size)
    g_w_down = jnp.concatenate([g_w_down_a, g_w_down_b], 0).astype(F32)
    g_w_up = jnp.concatenate([g_w_up_a, g_w_up_b], 1).astype(F32)
    y_own = (valid_own * (resid_own + mlp_own)).astype(BF16).reshape(n_rows, share_len, model_width)

    own_kv = own_share(flat_kv)
    grad_n1 = grad_n1 + times_transposed(own_kv, w_kv)
    normed_x1_own = own_share(normed_x1)
    x_grad_own = grad_resid + norm_back(grad_n1, normed_x1_own, own_share(inv_one), ln1_gain)
    x_grad_own = x_grad_own.reshape(n_rows, share_len, model_width)
    g_ln2_gain = jnp.sum(grad_n2 * normed_x2, axis=0)
    g_ln2_bias = jnp.sum(grad_n2, axis=0)
    g_b_out = jnp.sum(grad_resid_low.astype(F32), axis=0)
    g_b_down = jnp.sum(grad_y_own, axis=0)
    g_ln1_gain = jnp.sum(grad_n1 * normed_x1_own, axis=0)
    g_ln1_bias = jnp.sum(grad_n1, axis=0)
    g_b_up = jnp.sum(grad_pre.astype(F32), axis=0)
    g_b_query = jnp.sum(flat_query.astype(F32), axis=0) * q_scale
    g_b_value = jnp.sum(own_kv[:, head_size:].astype(F32), axis=0)
    owners = n_dp * n_seq
    small = jnp.stack([g_ln1_gain, g_ln1_bias, g_ln2_gain, g_ln2_bias, g_b_out, g_b_down])
    mine = (lax.iota(jnp.int32, n_tensor) == tensor_index).astype(F32)[:, None, None]
    query_piece = mine * jnp.moveaxis(g_b_query.reshape(num_heads, owners, -1), 1, 0).reshape(1, owners, -1)
    up_piece = mine * jnp.moveaxis(g_b_up.reshape(-1, owners, 128 // owners), 1, 0).reshape(1, owners, -1)
    small_piece = jnp.transpose(small.reshape(6, owners, n_tensor, -1), (2, 1, 0, 3)).reshape(n_tensor, owners, -1)
    value_piece = jnp.moveaxis(g_b_value.reshape(owners, n_tensor, -1), 1, 0)
    pieces = [query_piece, up_piece, small_piece, value_piece]
    sizes = [p.shape[-1] for p in pieces]
    room = -(-sum(sizes) // 1024) * 1024
    pieces.append(jnp.zeros((n_tensor, owners, room - sum(sizes)), F32))
    packed = jnp.concatenate(pieces, -1).reshape(2, 2, n_dp, n_seq, room // 128, 128)
    packed = sum_small(8, packed).reshape(-1)
    ends = [sum(sizes[: i + 1]) for i in range(len(sizes))]
    query_out, up_out, small_out, value_out = [packed[e - s : e] for s, e in zip(sizes, ends)]
    return (
        y_own,
        x_grad_own,
        g_w_query,
        query_out.reshape(num_heads, -1),
        g_w_kv,
        value_out,
        g_w_out,
        g_w_up,
        up_out.reshape(-1, 128 // owners),
        g_w_down,
        small_out.reshape(6, -1),
    )


def solution(mesh):
    placed = (
        P("dp", "seq", None),
        P("dp"),
        P("dp", ("seq", "tensor"), None),
        P(),
        P(),
        P(None, "tensor"),
        P("tensor"),
        P(),
        P(),
        P("tensor", None),
        P(),
        P(),
        P(),
        P(None, "tensor"),
        P("tensor"),
        P("tensor", None),
        P(),
    )
    return jax.shard_map(
        shards,
        mesh=mesh,
        in_specs=placed,
        out_specs=(
            P("dp", ("seq", "tensor"), None),
            P("dp", ("seq", "tensor"), None),
            P(("dp", "seq"), "tensor"),
            P("tensor", ("dp", "seq")),
            P(("dp", "seq", "tensor"), None),
            P(("dp", "seq", "tensor")),
            P("tensor", ("dp", "seq")),
            P(("dp", "seq"), "tensor"),
            P("tensor", ("dp", "seq")),
            P("tensor", ("dp", "seq")),
            P(None, ("dp", "seq", "tensor")),
        ),
        check_vma=False,
    )
```

```python
import functools
import math

import jax
import jax.numpy as jnp
from jax import lax
from jax.experimental import pallas as pl
from jax.experimental.pallas import tpu as pltpu
from jax.sharding import PartitionSpec as P

NORM_EPS = 1e-05
BF16 = jnp.bfloat16
F32 = jnp.float32
MESH = pl.DeviceIdType.MESH


def normalize(values_in):
    row_mean = jnp.mean(values_in, -1, keepdims=True)
    centered = values_in - row_mean
    variance = jnp.mean(centered * centered, -1, keepdims=True)
    inv_std = lax.rsqrt(variance + NORM_EPS)
    return (centered * inv_std, inv_std)


def norm_back(grad_in, normed, inv_std, norm_gain):
    scaled = grad_in * norm_gain
    mean_scaled = jnp.mean(scaled, -1, keepdims=True)
    mean_mixed = jnp.mean(scaled * normed, -1, keepdims=True)
    return inv_std * (scaled - mean_scaled - normed * mean_mixed)


def across_rows(left_in, right_in):
    return lax.dot_general(left_in, right_in, (((0,), (0,)), ((), ())), preferred_element_type=F32)


def times_transposed(left_in, right_in):
    return lax.dot_general(left_in, right_in, (((1,), (1,)), ((), ())), preferred_element_type=F32)


def tensor_partners():
    here = lax.axis_index("tensor")
    core = lax.rem(here, 2)
    chip = here // 2
    return here, chip, core, 2 * chip + 1 - core, 2 * (1 - chip) + core


def send(source, landing, send_sem, recv_sem, target):
    return pltpu.make_async_remote_copy(
        src_ref=source,
        dst_ref=landing,
        send_sem=send_sem,
        recv_sem=recv_sem,
        device_id={"tensor": target},
        device_id_type=MESH,
    )


def side_copies(plan, sources, landings, send_sems, recv_sems):
    _, dp_others = others_along("dp")
    copies = []
    for i, (source, row, rows, column, width) in enumerate(plan):
        for k, target in enumerate(dp_others):
            first = pl.multiple_of(target * width, width) if column is None else column
            window = sources[source].at[pl.ds(row, rows), pl.ds(first, width)]
            copies.append(remote(window, landings[i].at[k], send_sems.at[i, k], recv_sems.at[i, k], {"dp": target}))
    return copies


def greet_tensor_and_dp(with_dp):
    _, _, _, partner, across = tensor_partners()
    targets = [{"tensor": partner}, {"tensor": across}]
    if with_dp:
        targets += [{"dp": other} for other in others_along("dp")[1]]
    greet_all(targets)


def side_shapes(plan, sources):
    n_far = lax.axis_size("dp") - 1
    return [jax.ShapeDtypeStruct((n_far, rows, width), sources[i].dtype) for i, _, rows, _, width in plan]


def side_sems(plan):
    return [pltpu.SemaphoreType.DMA((max(len(plan), 1), max(lax.axis_size("dp") - 1, 1)))] * 2


def reduce_kernel(transposed, plan, n_sources, a_ref, w_ref, *refs):
    sources, o_ref, refs = refs[:n_sources], refs[n_sources], refs[n_sources + 1 :]
    landings, refs = refs[: len(plan)], refs[len(plan) :]
    w_here, part, core_out, core_in, over_out, over_in, w_sem, cs, cr, xs, xr, side_s, side_r = refs
    n_blocks, width = core_out.shape[0], core_out.shape[-1]
    share = o_ref.shape[0]
    _, chip, core, partner, across = tensor_partners()

    def load(n):
        where = pl.ds(n * width, width)
        block = w_ref.at[where, :] if transposed else w_ref.at[:, where]
        return pltpu.make_async_copy(block, w_here.at[n], w_sem.at[n])

    def to_partner(n):
        return send(core_out.at[n], core_in.at[n], cs.at[n], cr.at[n], partner)

    def to_across(n):
        return send(over_out.at[n], over_in.at[n], xs.at[n], xr.at[n], across)

    for n in range(n_blocks):
        load(n).start()
    greet_tensor_and_dp(len(plan) > 0)
    beside = side_copies(plan, sources, landings, side_s, side_r)
    for copy in beside:
        copy.start()

    def multiply(n):
        load(n).wait()
        slot = lax.rem(n, 2)
        dims = (((1,), (1,)), ((), ())) if transposed else (((1,), (0,)), ((), ()))
        product = lax.dot_general(a_ref[...], w_here[n], dims, preferred_element_type=F32)
        part[slot] = product.reshape(4, share, width)
        core_out[n, 0] = part[slot, 1 - core].astype(BF16)
        core_out[n, 1] = part[slot, 3 - core].astype(BF16)
        to_partner(n).start()

    def pass_on(n):
        slot = lax.rem(n, 2)
        to_partner(n).wait_recv()
        over_out[n] = (part[slot, 2 * (1 - chip) + core] + core_in[n, 1 - chip].astype(F32)).astype(BF16)
        to_across(n).start()
        columns = pl.ds(pl.multiple_of(n * width, width), width)
        o_ref[:, columns] = part[slot, 2 * chip + core] + core_in[n, chip].astype(F32)

    def step(n, carry):
        multiply(n)

        @pl.when(n > 0)
        def _():
            pass_on(n - 1)

        return carry

    lax.fori_loop(0, n_blocks, step, 0)
    pass_on(n_blocks - 1)

    def finish(n, carry):
        to_across(n).wait_recv()
        columns = pl.ds(pl.multiple_of(n * width, width), width)
        o_ref[:, columns] += over_in[n].astype(F32)
        to_across(n).wait_send()
        to_partner(n).wait_send()
        return carry

    lax.fori_loop(0, n_blocks, finish, 0)
    for copy in beside:
        copy.wait()


def product_to_owners(name, number, a, w, transposed, sources=(), plan=()):
    tokens, depth = a.shape
    model_width = w.shape[0] if transposed else w.shape[1]
    share = tokens // 4
    width = model_width // 4
    n_blocks = 4
    w_block = (n_blocks, width, depth) if transposed else (n_blocks, depth, width)
    dma = pltpu.SemaphoreType.DMA((n_blocks,))
    results = pl.pallas_call(
        functools.partial(reduce_kernel, transposed, plan, len(sources)),
        out_shape=[jax.ShapeDtypeStruct((share, model_width), F32)] + side_shapes(plan, sources),
        in_specs=[pl.BlockSpec(memory_space=pltpu.VMEM)] + [pl.BlockSpec(memory_space=pl.ANY)] * (1 + len(sources)),
        out_specs=[pl.BlockSpec(memory_space=pltpu.VMEM)] + [pl.BlockSpec(memory_space=pltpu.HBM)] * len(plan),
        scratch_shapes=[
            pltpu.VMEM(w_block, BF16),
            pltpu.VMEM((2, 4, share, width), F32),
            pltpu.VMEM((n_blocks, 2, share, width), BF16),
            pltpu.VMEM((n_blocks, 2, share, width), BF16),
            pltpu.VMEM((n_blocks, share, width), BF16),
            pltpu.VMEM((n_blocks, share, width), BF16),
            dma,
            dma,
            dma,
            dma,
            dma,
        ]
        + side_sems(plan),
        compiler_params=pltpu.CompilerParams(
            collective_id=number, has_side_effects=True, vmem_limit_bytes=40 * 1024 * 1024
        ),
        cost_estimate=estimate(25),
        name=name,
    )(a, w, *sources)
    return results[0] if not plan else results


def gather_kernel(plan, n_sources, own_ref, *refs):
    sources, o_ref, refs = refs[:n_sources], refs[n_sources], refs[n_sources + 1 :]
    landings, refs = refs[: len(plan)], refs[len(plan) :]
    cs, cr, xs, xr, fs, fr, side_s, side_r = refs
    n_chunks = cs.shape[0]
    share = own_ref.shape[0]
    rows = share // n_chunks
    here, _, _, partner, across = tensor_partners()

    def copy(source, owner, n, sems, target):
        where = pl.ds(n * rows, rows)
        return send(source.at[where], o_ref.at[owner, where], sems[0].at[n], sems[1].at[n], target)

    greet_tensor_and_dp(len(plan) > 0)
    beside = side_copies(plan, sources, landings, side_s, side_r)
    for n in range(n_chunks):
        copy(own_ref, here, n, (xs, xr), across).start()
    for side in beside:
        side.start()
    for n in range(n_chunks):
        copy(own_ref, here, n, (cs, cr), partner).start()
    o_ref[here] = own_ref[...]
    for n in range(n_chunks):
        copy(own_ref, here, n, (xs, xr), across).wait_recv()
        copy(o_ref.at[across], across, n, (fs, fr), partner).start()
    for n in range(n_chunks):
        copy(own_ref, here, n, (xs, xr), across).wait_send()
        copy(own_ref, here, n, (cs, cr), partner).wait()
        copy(o_ref.at[across], across, n, (fs, fr), partner).wait()
    for side in beside:
        side.wait()


def gather_shares(name, number, own, sources=(), plan=()):
    share, width = own.shape
    dma = pltpu.SemaphoreType.DMA((4,))
    results = pl.pallas_call(
        functools.partial(gather_kernel, plan, len(sources)),
        out_shape=[jax.ShapeDtypeStruct((4, share, width), own.dtype)] + side_shapes(plan, sources),
        in_specs=[pl.BlockSpec(memory_space=pltpu.VMEM)] + [pl.BlockSpec(memory_space=pl.ANY)] * len(sources),
        out_specs=[pl.BlockSpec(memory_space=pltpu.VMEM)] + [pl.BlockSpec(memory_space=pltpu.HBM)] * len(plan),
        scratch_shapes=[dma] * 6 + side_sems(plan),
        compiler_params=pltpu.CompilerParams(
            collective_id=number, has_side_effects=True, vmem_limit_bytes=16 * 1024 * 1024
        ),
        cost_estimate=estimate(20),
        name=name,
    )(own, *sources)
    return (results[0].reshape(4 * share, width), *results[1:])


def front_kernel(
    grad_ref, kv_ref, o_ref, all_ref, cs, cr, xs, xr, fs, fr, zs, zr, kcs, kcr, kxs, kxr, kfs, kfr
):
    n_chunks = cs.shape[0]
    rows = grad_ref.shape[0] // n_chunks
    here, _, _, partner, across = tensor_partners()
    seq_me, seq_others = others_along("seq")
    greet_all([{"tensor": partner}, {"tensor": across}] + [{"seq": other} for other in seq_others])

    def copy(source, owner, n, sems, target):
        where = pl.ds(n * rows, rows)
        return send(source.at[where], o_ref.at[owner, where], sems[0].at[n], sems[1].at[n], target)

    def to_seq(source, owner, target):
        return remote(source, all_ref.at[owner, here], zs.at[target], zr.at[owner], {"seq": target})

    def keys(source, seq, owner, sems, target):
        return send(source, all_ref.at[seq, owner], sems[0].at[seq], sems[1].at[seq], target)

    for other in seq_others:
        to_seq(kv_ref, seq_me, other).start()
    keys(kv_ref, seq_me, here, (kxs, kxr), across).start()
    keys(kv_ref, seq_me, here, (kcs, kcr), partner).start()
    for n in range(n_chunks):
        copy(grad_ref, here, n, (xs, xr), across).start()
    for n in range(n_chunks):
        copy(grad_ref, here, n, (cs, cr), partner).start()
    all_ref[seq_me, here] = kv_ref[...]
    o_ref[here] = grad_ref[...]
    for other in seq_others:
        remote(kv_ref, all_ref.at[other, here], zs.at[other], zr.at[other], {"seq": other}).wait_recv()
        keys(all_ref.at[other, here], other, here, (kxs, kxr), across).start()
        keys(all_ref.at[other, here], other, here, (kcs, kcr), partner).start()
    keys(kv_ref, seq_me, across, (kxs, kxr), across).wait_recv()
    keys(all_ref.at[seq_me, across], seq_me, across, (kfs, kfr), partner).start()
    for n in range(n_chunks):
        copy(grad_ref, here, n, (xs, xr), across).wait_recv()
        copy(o_ref.at[across], across, n, (fs, fr), partner).start()
    for other in seq_others:
        keys(kv_ref, other, across, (kxs, kxr), across).wait_recv()
        keys(all_ref.at[other, across], other, across, (kfs, kfr), partner).start()
    for n in range(n_chunks):
        copy(grad_ref, here, n, (xs, xr), across).wait_send()
        copy(grad_ref, here, n, (cs, cr), partner).wait()
        copy(o_ref.at[across], across, n, (fs, fr), partner).wait()
    for other in seq_others:
        to_seq(kv_ref, seq_me, other).wait_send()
    for seq in [seq_me] + seq_others:
        keys(kv_ref, seq, here, (kxs, kxr), across).wait_send()
        keys(kv_ref, seq, here, (kcs, kcr), partner).wait()
        keys(all_ref.at[seq, across], seq, across, (kfs, kfr), partner).wait()


def front(number, grad_own, kv_own):
    n_seq = lax.axis_size("seq")
    share, width = grad_own.shape
    dma = pltpu.SemaphoreType.DMA
    vmem = pl.BlockSpec(memory_space=pltpu.VMEM)
    grads, kv_all = pl.pallas_call(
        front_kernel,
        out_shape=(
            jax.ShapeDtypeStruct((4, share, width), BF16),
            jax.ShapeDtypeStruct((n_seq, 4) + kv_own.shape, BF16),
        ),
        in_specs=[vmem] * 2,
        out_specs=(vmem,) * 2,
        scratch_shapes=[dma((4,))] * 6 + [dma((n_seq,))] * 8,
        compiler_params=pltpu.CompilerParams(
            collective_id=number, has_side_effects=True, vmem_limit_bytes=16 * 1024 * 1024
        ),
        cost_estimate=estimate(30),
        name="front",
    )(grad_own, kv_own)
    return grads.reshape(4 * share, width), kv_all


def remote(source, landing, send_sem, recv_sem, target):
    return pltpu.make_async_remote_copy(
        src_ref=source,
        dst_ref=landing,
        send_sem=send_sem,
        recv_sem=recv_sem,
        device_id=target,
        device_id_type=MESH,
    )


def greet_all(targets):
    barrier = pltpu.get_barrier_semaphore()
    for target in targets:
        pl.semaphore_signal(barrier, inc=1, device_id=target, device_id_type=MESH)
    pl.semaphore_wait(barrier, len(targets))


def others_along(axis):
    size = lax.axis_size(axis)
    me = lax.axis_index(axis)
    return me, [lax.rem(me + k, size) for k in range(1, size)]


def small_kernel(in_ref, o_ref, core_in, over_out, over_in, dp_out, dp_in, seq_out, seq_in, cs, cr, xs, xr, ys, yr, zs, zr):
    _, chip, core, partner, across = tensor_partners()
    dp_me, dp_others = others_along("dp")
    seq_me, seq_others = others_along("seq")
    greet_all(
        [{"tensor": partner}, {"tensor": across}]
        + [{"dp": other} for other in dp_others]
        + [{"seq": other} for other in seq_others]
    )

    def to_partner(j):
        return remote(in_ref.at[j, 1 - core], core_in.at[j], cs.at[j], cr.at[j], {"tensor": partner})

    to_partner(0).start()
    to_partner(1).start()
    to_partner(0).wait()
    to_partner(1).wait()
    over_out[...] = in_ref[1 - chip, core] + core_in[1 - chip]
    to_across = remote(over_out, over_in, xs.at[0], xr.at[0], {"tensor": across})
    to_across.start()
    to_across.wait()
    dp_out[...] = in_ref[chip, core] + core_in[chip] + over_in[...]

    def fold(outgoing, incoming, send_sems, recv_sems, axis, me, others):
        def copy(target):
            return remote(outgoing.at[target], incoming.at[me], send_sems.at[target], recv_sems.at[me], {axis: target})

        for other in others:
            copy(other).start()
        total = outgoing[me]
        for other in others:
            remote(
                outgoing.at[other], incoming.at[other], send_sems.at[other], recv_sems.at[other], {axis: other}
            ).wait_recv()
            total = total + incoming[other]
        for other in others:
            copy(other).wait_send()
        return total

    seq_out[...] = fold(dp_out, dp_in, ys, yr, "dp", dp_me, dp_others)
    o_ref[...] = fold(seq_out, seq_in, zs, zr, "seq", seq_me, seq_others)


def sum_small(number, packed):
    n_dp, n_seq, rows, lanes = packed.shape[2:]
    dma = pltpu.SemaphoreType.DMA
    return pl.pallas_call(
        small_kernel,
        out_shape=jax.ShapeDtypeStruct((rows, lanes), F32),
        in_specs=[pl.BlockSpec(memory_space=pltpu.VMEM)],
        out_specs=pl.BlockSpec(memory_space=pltpu.VMEM),
        scratch_shapes=[
            pltpu.VMEM((2, n_dp, n_seq, rows, lanes), F32),
            pltpu.VMEM((n_dp, n_seq, rows, lanes), F32),
            pltpu.VMEM((n_dp, n_seq, rows, lanes), F32),
            pltpu.VMEM((n_dp, n_seq, rows, lanes), F32),
            pltpu.VMEM((n_dp, n_seq, rows, lanes), F32),
            pltpu.VMEM((n_seq, rows, lanes), F32),
            pltpu.VMEM((n_seq, rows, lanes), F32),
            dma((2,)),
            dma((2,)),
            dma((1,)),
            dma((1,)),
            dma((n_dp,)),
            dma((n_dp,)),
            dma((n_seq,)),
            dma((n_seq,)),
        ],
        compiler_params=pltpu.CompilerParams(collective_id=number, has_side_effects=True),
        cost_estimate=estimate(12),
        name="sum_small",
    )(packed)


def kv_kernel(plan, n_sources, g_ref, two_ref, *refs):
    sources, o_ref, two_all, refs = refs[:n_sources], refs[n_sources], refs[n_sources + 1], refs[n_sources + 2 :]
    landings, refs = refs[: len(plan)], refs[len(plan) :]
    core_in, over_out, over_in, seq_out, seq_in, own = refs[:6]
    cs, cr, xs, xr, zs, zr, gs, gr, ts, tr, side_s, side_r = refs[6:]
    here, chip, core, partner, across = tensor_partners()
    seq_me, seq_others = others_along("seq")
    greet_all(
        [{"tensor": partner}, {"tensor": across}]
        + [{"seq": other} for other in seq_others]
        + [{"dp": other} for other in others_along("dp")[1]]
    )
    beside = side_copies(plan, sources, landings, side_s, side_r)
    for copy in beside:
        copy.start()

    def two_copy(source, owner, i, target):
        return remote(source, two_all.at[owner], ts.at[i], tr.at[i], {"tensor": target})

    def to_partner(j):
        return remote(g_ref.at[2 * j + 1 - core], core_in.at[j], cs.at[j], cr.at[j], {"tensor": partner})

    to_partner(1 - chip).start()
    to_partner(chip).start()
    to_partner(1 - chip).wait()
    over_out[...] = (g_ref[2 * (1 - chip) + core].astype(F32) + core_in[1 - chip].astype(F32)).astype(BF16)
    to_across = remote(over_out, over_in, xs.at[0], xr.at[0], {"tensor": across})
    to_across.start()
    two_copy(two_ref, here, 0, across).start()
    two_copy(two_ref, here, 1, partner).start()
    two_all[here] = two_ref[...]
    to_partner(chip).wait()
    to_across.wait()
    seq_out[...] = (
        g_ref[2 * chip + core].astype(F32) + core_in[chip].astype(F32) + over_in[...].astype(F32)
    ).astype(BF16)

    def to_seq(target):
        return remote(seq_out.at[target], seq_in.at[seq_me], zs.at[target], zr.at[seq_me], {"seq": target})

    for other in seq_others:
        to_seq(other).start()
    two_copy(two_ref, across, 0, across).wait_recv()
    two_copy(two_all.at[across], across, 2, partner).start()
    total = seq_out[seq_me].astype(F32)
    for other in seq_others:
        remote(seq_out.at[other], seq_in.at[other], zs.at[other], zr.at[other], {"seq": other}).wait_recv()
        total = total + seq_in[other].astype(F32)
    own[...] = total.astype(BF16)
    o_ref[here] = own[...]
    x_copy = remote(own, o_ref.at[here], gs.at[0], gr.at[0], {"tensor": across})
    c_copy = remote(own, o_ref.at[here], gs.at[1], gr.at[1], {"tensor": partner})
    x_copy.start()
    c_copy.start()
    x_copy.wait_recv()
    f_copy = remote(o_ref.at[across], o_ref.at[across], gs.at[2], gr.at[2], {"tensor": partner})
    f_copy.start()
    x_copy.wait_send()
    c_copy.wait()
    f_copy.wait()
    for other in seq_others:
        to_seq(other).wait_send()
    two_copy(two_ref, here, 0, across).wait_send()
    two_copy(two_ref, here, 1, partner).wait()
    two_copy(two_all.at[across], across, 2, partner).wait()
    for copy in beside:
        copy.wait()


def sum_grad_kv(number, parts, two_own, sources, plan):
    _, n_seq, share, width = parts.shape
    dma = pltpu.SemaphoreType.DMA
    vmem = pl.BlockSpec(memory_space=pltpu.VMEM)
    results = pl.pallas_call(
        functools.partial(kv_kernel, plan, len(sources)),
        out_shape=[
            jax.ShapeDtypeStruct((4, share, width), BF16),
            jax.ShapeDtypeStruct((4,) + two_own.shape, BF16),
        ]
        + side_shapes(plan, sources),
        in_specs=[vmem] * 2 + [pl.BlockSpec(memory_space=pl.ANY)] * len(sources),
        out_specs=[vmem] * 2 + [pl.BlockSpec(memory_space=pltpu.HBM)] * len(plan),
        scratch_shapes=[
            pltpu.VMEM((2, n_seq, share, width), BF16),
            pltpu.VMEM((n_seq, share, width), BF16),
            pltpu.VMEM((n_seq, share, width), BF16),
            pltpu.VMEM((n_seq, share, width), BF16),
            pltpu.VMEM((n_seq, share, width), BF16),
            pltpu.VMEM((share, width), BF16),
            dma((2,)),
            dma((2,)),
            dma((1,)),
            dma((1,)),
            dma((n_seq,)),
            dma((n_seq,)),
            dma((3,)),
            dma((3,)),
            dma((3,)),
            dma((3,)),
        ]
        + side_sems(plan),
        compiler_params=pltpu.CompilerParams(
            collective_id=number, has_side_effects=True, vmem_limit_bytes=32 * 1024 * 1024
        ),
        cost_estimate=estimate(30),
        name="sum_grad_kv",
    )(parts, two_own, *sources)
    return (results[0].reshape(4 * share, width), *results[1:])


def estimate(microseconds):
    return pl.CostEstimate(flops=int(microseconds * 1e6), bytes_accessed=0, transcendentals=0)


def attention_kernel(len_ref, q_ref, kv_ref, o_ref, lse_ref, scores):
    share = o_ref.shape[0] // 4
    n_rows = len_ref.shape[0]
    tile = share // n_rows
    block = 4 * tile
    head = kv_ref.shape[-1] // 2
    heads = q_ref.shape[1] // head
    lanes = heads * tile
    seq_me = lax.axis_index("seq")

    def one_tile(t, carry):
        quarter = t // n_rows
        row = t - quarter * n_rows
        length = len_ref[row]
        first = seq_me * block + quarter * tile
        where = pl.ds(pl.multiple_of(t * tile, tile), tile)
        own_rows = pl.ds(pl.multiple_of(row * tile, tile), tile)

        @pl.when(first >= length)
        def _():
            o_ref[where, :] = jnp.zeros((tile, heads * head), BF16)
            lse_ref[t] = jnp.zeros((1, lanes), F32)

        @pl.when(first < length)
        def _():
            queries = q_ref[where, :]
            stacked = jnp.concatenate([queries[:, h * head : (h + 1) * head] for h in range(heads)], 0)
            n_blocks = jnp.minimum(seq_me + 1, (length + block - 1) // block)
            place = first + lax.rem(lax.broadcasted_iota(jnp.int32, (1, lanes), 1), tile)
            limit = jnp.minimum(place + 1, length)
            key_index = lax.broadcasted_iota(jnp.int32, (block, lanes), 0)

            def score(b, highest):
                keys = kv_ref[b, :, own_rows, :head].reshape(block, head)
                s = lax.dot_general(keys, stacked, (((1,), (1,)), ((), ())), preferred_element_type=F32)
                s = jnp.where(key_index < limit - b * block, s, -1e30)
                scores[b] = s
                return jnp.maximum(highest, jnp.max(s, 0, keepdims=True))

            highest = lax.fori_loop(0, n_blocks, score, jnp.full((1, lanes), -1e30, F32))

            def mix(b, both):
                total, mixed = both
                values = kv_ref[b, :, own_rows, head:].reshape(block, head)
                p = jnp.exp(scores[b] - highest)
                total = total + jnp.sum(p, 0, keepdims=True)
                mixed = mixed + lax.dot_general(
                    values, p.astype(BF16), (((0,), (0,)), ((), ())), preferred_element_type=F32
                )
                return total, mixed

            total, mixed = lax.fori_loop(
                0, n_blocks, mix, (jnp.zeros((1, lanes), F32), jnp.zeros((head, lanes), F32))
            )
            lse_ref[t] = highest + jnp.log(total)
            back = jnp.transpose(mixed / total)
            o_ref[where, :] = jnp.concatenate(
                [back[h * tile : (h + 1) * tile] for h in range(heads)], 1
            ).astype(BF16)

        return carry

    lax.fori_loop(0, 4 * n_rows, one_tile, 0)


def attention(lengths, queries, kv_all):
    tokens, width = queries.shape
    n_rows = lengths.shape[0]
    n_seq, kv_width = kv_all.shape[0], kv_all.shape[-1]
    tile = tokens // (4 * n_rows)
    lanes = width // (kv_width // 2) * tile
    return pl.pallas_call(
        attention_kernel,
        out_shape=(
            jax.ShapeDtypeStruct((tokens, width), BF16),
            jax.ShapeDtypeStruct((4 * n_rows, 1, lanes), F32),
        ),
        in_specs=[pl.BlockSpec(memory_space=pltpu.SMEM)] + [pl.BlockSpec(memory_space=pltpu.VMEM)] * 2,
        out_specs=(pl.BlockSpec(memory_space=pltpu.VMEM),) * 2,
        scratch_shapes=[pltpu.VMEM((n_seq, 4 * tile, lanes), F32)],
        compiler_params=pltpu.CompilerParams(vmem_limit_bytes=24 * 1024 * 1024),
        cost_estimate=estimate(10),
        name="attention",
    )(lengths, queries, kv_all)


def attention_back_kernel(len_ref, q_ref, do_ref, kv_ref, lse_ref, dq_ref, dkv_ref, probs, grads, total, keys_t):
    share = dq_ref.shape[0] // 4
    n_rows = len_ref.shape[0]
    tile = share // n_rows
    block = 4 * tile
    head = kv_ref.shape[-1] // 2
    heads = q_ref.shape[1] // head
    lanes = heads * tile
    n_seq = total.shape[0]
    seq_me = lax.axis_index("seq")

    def one_row(row, carry):
        length = len_ref[row]
        n_blocks = jnp.minimum(seq_me + 1, (length + block - 1) // block)
        total[...] = jnp.zeros_like(total)
        own_rows = pl.ds(pl.multiple_of(row * tile, tile), tile)
        for b in range(n_seq):
            keys_t[b] = jnp.transpose(kv_ref[b, :, own_rows, :head].reshape(block, head).astype(F32)).astype(BF16)

        def one_tile(quarter, carry):
            t = quarter * n_rows + row
            first = seq_me * block + quarter * tile
            where = pl.ds(pl.multiple_of(t * tile, tile), tile)

            @pl.when(first >= length)
            def _():
                dq_ref[where, :] = jnp.zeros((tile, heads * head), BF16)

            @pl.when(first < length)
            def _():
                def stack(ref):
                    rows = ref[where, :]
                    return jnp.concatenate([rows[:, h * head : (h + 1) * head] for h in range(heads)], 0)

                stacked = stack(q_ref)
                outer = stack(do_ref)
                lse = lse_ref[t]
                place = first + lax.rem(lax.broadcasted_iota(jnp.int32, (1, lanes), 1), tile)
                limit = jnp.minimum(place + 1, length)
                key_index = lax.broadcasted_iota(jnp.int32, (block, lanes), 0)

                def score(b, inner):
                    keys = kv_ref[b, :, own_rows, :head].reshape(block, head)
                    values = kv_ref[b, :, own_rows, head:].reshape(block, head)
                    s = lax.dot_general(keys, stacked, (((1,), (1,)), ((), ())), preferred_element_type=F32)
                    p = jnp.where(key_index < limit - b * block, jnp.exp(s - lse), 0.0)
                    g = lax.dot_general(values, outer, (((1,), (1,)), ((), ())), preferred_element_type=F32)
                    probs[b] = p
                    grads[b] = g
                    total[b, :, head:] += jnp.dot(p.astype(BF16), outer, preferred_element_type=F32)
                    return inner + jnp.sum(p * g, 0, keepdims=True)

                inner = lax.fori_loop(0, n_blocks, score, jnp.zeros((1, lanes), F32))

                def back(b, dq):
                    ds = (probs[b] * (grads[b] - inner)).astype(BF16)
                    total[b, :, :head] += jnp.dot(ds, stacked, preferred_element_type=F32)
                    return dq + jnp.dot(keys_t[b], ds, preferred_element_type=F32)

                dq = jnp.transpose(lax.fori_loop(0, n_blocks, back, jnp.zeros((head, lanes), F32)))
                dq_ref[where, :] = jnp.concatenate(
                    [dq[h * tile : (h + 1) * tile] for h in range(heads)], 1
                ).astype(BF16)

            return carry

        lax.fori_loop(0, 4, one_tile, 0)
        for quarter in range(4):
            for b in range(n_seq):
                dkv_ref[quarter, b, own_rows, :] = total[b, quarter * tile : (quarter + 1) * tile, :].astype(BF16)
        return carry

    lax.fori_loop(0, n_rows, one_row, 0)


def attention_back(lengths, queries, grad_mixed, kv_all, lse):
    tokens, width = queries.shape
    n_rows = lengths.shape[0]
    n_seq, kv_width = kv_all.shape[0], kv_all.shape[-1]
    tile = tokens // (4 * n_rows)
    lanes = width // (kv_width // 2) * tile
    block = 4 * tile
    return pl.pallas_call(
        attention_back_kernel,
        out_shape=(
            jax.ShapeDtypeStruct((tokens, width), BF16),
            jax.ShapeDtypeStruct((4, n_seq, tokens // 4, kv_width), BF16),
        ),
        in_specs=[pl.BlockSpec(memory_space=pltpu.SMEM)] + [pl.BlockSpec(memory_space=pltpu.VMEM)] * 4,
        out_specs=(pl.BlockSpec(memory_space=pltpu.VMEM),) * 2,
        scratch_shapes=[
            pltpu.VMEM((n_seq, block, lanes), F32),
            pltpu.VMEM((n_seq, block, lanes), F32),
            pltpu.VMEM((n_seq, block, kv_width), F32),
            pltpu.VMEM((n_seq, kv_width // 2, block), BF16),
        ],
        compiler_params=pltpu.CompilerParams(vmem_limit_bytes=32 * 1024 * 1024),
        cost_estimate=estimate(25),
        name="attention_back",
    )(lengths, queries, grad_mixed, kv_all, lse)


def last_kernel(
    q_ref, kv_ref, out_ref, q_sum, kv_sum, out_sum,
    packed, dp_in, near_out, near_in, far_out, far_in, total, ys, yr, ns, nr, fs, fr,
):
    rows = q_ref.shape[2]
    kv_rows, kv_width = kv_ref.shape[3:]
    per_line = q_ref.shape[3] // kv_width
    lines = kv_rows // per_line
    here = lax.axis_index("tensor")
    dp_me, dp_others = others_along("dp")
    seq_me = lax.axis_index("seq")
    beside = seq_me + 1 - 2 * lax.rem(seq_me, 2)
    far = seq_me + 2 - 4 * (seq_me // 2)
    opposite = 3 - seq_me
    greet_all([{"dp": other} for other in dp_others] + [{"seq": beside}, {"seq": far}])

    def to_dp(k, b):
        return remote(packed.at[dp_others[k], b], dp_in.at[k, b], ys.at[k, b], yr.at[k, b], {"dp": dp_others[k]})

    def pack(d, b):
        packed[d, b, :rows] = q_ref[d, b]
        packed[d, b, rows : 2 * rows] = out_ref[d, b]
        for i in range(per_line):
            packed[d, b, 2 * rows :, i * kv_width : (i + 1) * kv_width] = kv_ref[
                d, b, here, i * lines : (i + 1) * lines
            ]

    order = (beside, opposite, far, seq_me)
    for b in order:
        for k, d in enumerate(dp_others):
            pack(d, b)
            to_dp(k, b).start()
    for b in order:
        pack(dp_me, b)

    def summed(b):
        value = packed[dp_me, b].astype(F32)
        for k in range(len(dp_others)):
            to_dp(k, b).wait_recv()
            value = value + dp_in[k, b].astype(F32)
        return value

    def to_beside(i):
        return remote(near_out.at[i], near_in.at[i], ns.at[i], nr.at[i], {"seq": beside})

    near_out[0] = summed(beside).astype(BF16)
    near_out[1] = summed(opposite).astype(BF16)
    to_beside(1).start()
    to_beside(0).start()
    total[...] = summed(far)
    to_beside(1).wait_recv()
    far_out[...] = (total[...] + near_in[1].astype(F32)).astype(BF16)
    to_far = remote(far_out, far_in, fs.at[0], fr.at[0], {"seq": far})
    to_far.start()
    total[...] = summed(seq_me)
    to_beside(0).wait_recv()
    total[...] += near_in[0].astype(F32)
    to_far.wait_recv()
    total[...] += far_in[...].astype(F32)
    q_sum[...] = total[:rows]
    out_sum[...] = jnp.transpose(total[rows : 2 * rows])
    for i in range(per_line):
        kv_sum[i * lines : (i + 1) * lines] = total[2 * rows :, i * kv_width : (i + 1) * kv_width]
    for b in order:
        for k in range(len(dp_others)):
            to_dp(k, b).wait_send()
    to_beside(0).wait_send()
    to_beside(1).wait_send()
    to_far.wait_send()


def sum_last(number, q_part, kv_part, out_part):
    n_dp, n_seq, rows, width = q_part.shape
    kv_rows, kv_width = kv_part.shape[3:]
    block = (2 * rows + kv_rows * kv_width // width, width)
    n_far = n_dp - 1
    dma = pltpu.SemaphoreType.DMA
    vmem = pl.BlockSpec(memory_space=pltpu.VMEM)
    return pl.pallas_call(
        last_kernel,
        out_shape=(
            jax.ShapeDtypeStruct((rows, width), F32),
            jax.ShapeDtypeStruct((kv_rows, kv_width), F32),
            jax.ShapeDtypeStruct((width, rows), F32),
        ),
        in_specs=[vmem] * 3,
        out_specs=(vmem,) * 3,
        scratch_shapes=[
            pltpu.VMEM((n_dp, n_seq) + block, BF16),
            pltpu.VMEM((n_far, n_seq) + block, BF16),
            pltpu.VMEM((2,) + block, BF16),
            pltpu.VMEM((2,) + block, BF16),
            pltpu.VMEM(block, BF16),
            pltpu.VMEM(block, BF16),
            pltpu.VMEM(block, F32),
            dma((n_far, n_seq)),
            dma((n_far, n_seq)),
            dma((2,)),
            dma((2,)),
            dma((1,)),
            dma((1,)),
        ],
        compiler_params=pltpu.CompilerParams(
            collective_id=number, has_side_effects=True, vmem_limit_bytes=48 * 1024 * 1024
        ),
        cost_estimate=estimate(70),
        name="sum_last",
    )(q_part, kv_part, out_part)


def shards(
    layer_input,
    lengths,
    cotangent,
    ln1_gain,
    ln1_bias,
    w_query,
    b_query,
    w_kv,
    b_value,
    w_out,
    b_out,
    ln2_gain,
    ln2_bias,
    w_up,
    b_up,
    w_down,
    b_down,
):
    n_rows, seq_len, model_width = layer_input.shape
    n_tensor = lax.axis_size("tensor")
    n_dp = lax.axis_size("dp")
    n_seq = lax.axis_size("seq")
    share_len = seq_len // n_tensor
    tensor_index = lax.axis_index("tensor")
    seq_index = lax.axis_index("seq")
    head_size = w_kv.shape[1] // 2
    num_heads = w_query.shape[1] // head_size
    q_scale = 1.0 / math.sqrt(head_size)
    n_tok = n_rows * seq_len
    n_own = n_rows * share_len

    def by_share(values_in):
        return jnp.moveaxis(values_in.reshape((n_rows, n_tensor, share_len) + values_in.shape[2:]), 1, 0)

    def own_share(values_in):
        return lax.dynamic_index_in_dim(values_in.reshape((n_tensor, n_own) + values_in.shape[1:]), tensor_index, 0, False)

    positions = seq_index * seq_len + jnp.arange(seq_len, dtype=jnp.int32)
    is_valid = (positions[None, :] < lengths[:, None]).astype(F32)
    valid_own = own_share(by_share(is_valid).reshape(n_tok))[:, None]
    grad_y_own = cotangent.reshape(n_own, model_width).astype(F32) * valid_own
    x_float = by_share(layer_input).reshape(n_tok, model_width).astype(F32)
    normed_x1, inv_one = normalize(x_float)
    flat_one = (normed_x1 * ln1_gain + ln1_bias).astype(BF16)
    kv_bias = jnp.concatenate([jnp.zeros((head_size,), F32), b_value.astype(F32)])
    kv_own = (jnp.dot(own_share(flat_one), w_kv, preferred_element_type=F32) + kv_bias).astype(BF16)
    queries = ((jnp.dot(flat_one, w_query, preferred_element_type=F32) + b_query) * q_scale).astype(BF16)
    grad_y_low, kv_all = front(0, grad_y_own.astype(BF16), kv_own)

    half_width = model_width // n_dp
    hidden = w_up.shape[1]
    chunk = hidden // 8
    dp_me = lax.axis_index("dp")

    def own_columns(values_in):
        return lax.dynamic_slice_in_dim(values_in, dp_me * half_width, half_width, 1)

    mixed_heads, log_total = attention(lengths, queries, kv_all)
    attn_own, grad_y_far_a = product_to_owners(
        "attn_out", 1, mixed_heads, w_out, False, (grad_y_low,), ((0, 0, n_tok // 2, None, half_width),)
    )
    x_own = own_share(x_float)
    resid_own = x_own + (attn_own + b_out)
    normed_x2, inv_two = normalize(resid_own)
    normed_two = (normed_x2 * ln2_gain + ln2_bias).astype(BF16)
    flat_two, grad_y_far_b = gather_shares(
        "gather_norm_two", 2, normed_two, (grad_y_low,), ((0, n_tok // 2, n_tok // 2, None, half_width),)
    )
    pre_act = jnp.dot(flat_two, w_up, preferred_element_type=F32) + b_up
    activated, gelu_pull = jax.vjp(lambda inner_in: jax.nn.gelu(inner_in, approximate=True), pre_act)
    act_low = activated.astype(BF16)
    grad_act = times_transposed(grad_y_low, w_down)
    grad_pre = gelu_pull(grad_act)[0].astype(BF16)

    def window(source, first, count):
        return (source, 0, n_tok, first * chunk, count * chunk)

    grad_n2, act_far_a, two_far_own = product_to_owners(
        "grad_norm_two", 3, grad_pre, w_up, True, (act_low, normed_two), (window(0, 0, 3), (1, 0, n_own, None, half_width))
    )
    grad_resid = grad_y_own + norm_back(grad_n2, normed_x2, inv_two, ln2_gain)
    grad_resid_low = grad_resid.astype(BF16)
    flat_resid, act_far_b = gather_shares("gather_grad_resid", 4, grad_resid_low, (act_low,), (window(0, 3, 3),))
    grad_mixed = times_transposed(flat_resid, w_out).astype(BF16)
    flat_query, grad_kv = attention_back(lengths, queries, grad_mixed, kv_all, log_total)
    grad_n1, act_far_c, pre_far_a = product_to_owners(
        "grad_norm_one", 6, flat_query, w_query, True, (act_low, grad_pre), (window(0, 6, 2), window(1, 0, 1))
    )
    grad_n1 = grad_n1 * q_scale
    two_swapped = jnp.swapaxes(two_far_own, 0, 1).reshape(n_own, -1)
    flat_kv, two_far, pre_far_b = sum_grad_kv(7, grad_kv, two_swapped, (grad_pre,), (window(0, 1, 4),))
    mlp_own, pre_far_c = product_to_owners("mlp_out", 5, act_low, w_down, False, (grad_pre, flat_kv), (window(0, 5, 3),))
    mlp_own = mlp_own + b_down

    grad_y_far = jnp.concatenate([grad_y_far_a, grad_y_far_b], 1)
    grad_y_here = own_columns(grad_y_low)
    two_here = own_columns(flat_two)
    two_far = two_far.reshape(n_tok, n_dp - 1, half_width)

    def part_down(first, count, far):
        total = across_rows(act_low[:, first * chunk : (first + count) * chunk], grad_y_here)
        for k in range(n_dp - 1):
            total = total + across_rows(far[k], grad_y_far[k])
        return lax.psum_scatter(total.astype(BF16), "seq", scatter_dimension=1, tiled=True)

    def part_up(first, count, fars):
        total = across_rows(two_here, grad_pre[:, first * chunk : (first + count) * chunk])
        for k in range(n_dp - 1):
            far = jnp.concatenate([piece[k] for piece in fars], 1) if len(fars) > 1 else fars[0][k]
            total = total + across_rows(two_far[:, k], far)
        return lax.psum_scatter(total.astype(BF16), "seq", scatter_dimension=0, tiled=True)

    g_w_down = jnp.concatenate([part_down(0, 3, act_far_a), part_down(3, 3, act_far_b), part_down(6, 2, act_far_c)], 0)
    g_w_up = jnp.concatenate([part_up(0, 5, (pre_far_a, pre_far_b)), part_up(5, 3, (pre_far_c,))], 1)
    g_w_down = g_w_down.astype(F32)
    g_w_up = g_w_up.astype(F32)

    def by_owner(values_in, *between):
        return values_in.astype(BF16).reshape((n_dp, n_seq) + between + (-1, values_in.shape[1]))

    q_part = by_owner(across_rows(flat_one, flat_query) * q_scale)
    kv_part = by_owner(across_rows(flat_one, flat_kv), n_tensor)
    out_part = by_owner(across_rows(flat_resid, mixed_heads))
    g_w_query, g_w_kv, g_w_out = sum_last(9, q_part, kv_part, out_part)
    y_own = (valid_own * (resid_own + mlp_own)).astype(BF16).reshape(n_rows, share_len, model_width)

    own_kv = own_share(flat_kv)
    grad_n1 = grad_n1 + times_transposed(own_kv, w_kv)
    normed_x1_own = own_share(normed_x1)
    x_grad_own = grad_resid + norm_back(grad_n1, normed_x1_own, own_share(inv_one), ln1_gain)
    x_grad_own = x_grad_own.reshape(n_rows, share_len, model_width)
    g_ln2_gain = jnp.sum(grad_n2 * normed_x2, axis=0)
    g_ln2_bias = jnp.sum(grad_n2, axis=0)
    g_b_out = jnp.sum(grad_resid_low.astype(F32), axis=0)
    g_b_down = jnp.sum(grad_y_own, axis=0)
    g_ln1_gain = jnp.sum(grad_n1 * normed_x1_own, axis=0)
    g_ln1_bias = jnp.sum(grad_n1, axis=0)
    g_b_up = jnp.sum(grad_pre.astype(F32), axis=0)
    g_b_query = jnp.sum(flat_query.astype(F32), axis=0) * q_scale
    g_b_value = jnp.sum(own_kv[:, head_size:].astype(F32), axis=0)
    owners = n_dp * n_seq
    small = jnp.stack([g_ln1_gain, g_ln1_bias, g_ln2_gain, g_ln2_bias, g_b_out, g_b_down])
    mine = (lax.iota(jnp.int32, n_tensor) == tensor_index).astype(F32)[:, None, None]
    query_piece = mine * jnp.moveaxis(g_b_query.reshape(num_heads, owners, -1), 1, 0).reshape(1, owners, -1)
    up_piece = mine * jnp.moveaxis(g_b_up.reshape(-1, owners, 128 // owners), 1, 0).reshape(1, owners, -1)
    small_piece = jnp.transpose(small.reshape(6, owners, n_tensor, -1), (2, 1, 0, 3)).reshape(n_tensor, owners, -1)
    value_piece = jnp.moveaxis(g_b_value.reshape(owners, n_tensor, -1), 1, 0)
    pieces = [query_piece, up_piece, small_piece, value_piece]
    sizes = [p.shape[-1] for p in pieces]
    room = -(-sum(sizes) // 1024) * 1024
    pieces.append(jnp.zeros((n_tensor, owners, room - sum(sizes)), F32))
    packed = jnp.concatenate(pieces, -1).reshape(2, 2, n_dp, n_seq, room // 128, 128)
    packed = sum_small(8, packed).reshape(-1)
    ends = [sum(sizes[: i + 1]) for i in range(len(sizes))]
    query_out, up_out, small_out, value_out = [packed[e - s : e] for s, e in zip(sizes, ends)]
    return (
        y_own,
        x_grad_own,
        g_w_query,
        query_out.reshape(num_heads, -1),
        g_w_kv,
        value_out,
        g_w_out,
        g_w_up,
        up_out.reshape(-1, 128 // owners),
        g_w_down,
        small_out.reshape(6, -1),
    )


def solution(mesh):
    placed = (
        P("dp", "seq", None),
        P("dp"),
        P("dp", ("seq", "tensor"), None),
        P(),
        P(),
        P(None, "tensor"),
        P("tensor"),
        P(),
        P(),
        P("tensor", None),
        P(),
        P(),
        P(),
        P(None, "tensor"),
        P("tensor"),
        P("tensor", None),
        P(),
    )
    return jax.shard_map(
        shards,
        mesh=mesh,
        in_specs=placed,
        out_specs=(
            P("dp", ("seq", "tensor"), None),
            P("dp", ("seq", "tensor"), None),
            P(("dp", "seq"), "tensor"),
            P("tensor", ("dp", "seq")),
            P(("dp", "seq", "tensor"), None),
            P(("dp", "seq", "tensor")),
            P("tensor", ("dp", "seq")),
            P(("dp", "seq"), "tensor"),
            P("tensor", ("dp", "seq")),
            P("tensor", ("dp", "seq")),
            P(None, ("dp", "seq", "tensor")),
        ),
        check_vma=False,
    )
```

```python
import functools
import math

import jax
import jax.numpy as jnp
from jax import lax
from jax.experimental import pallas as pl
from jax.experimental.pallas import tpu as pltpu
from jax.sharding import PartitionSpec as P

NORM_EPS = 1e-05
BF16 = jnp.bfloat16
F32 = jnp.float32
MESH = pl.DeviceIdType.MESH


def normalize(values_in):
    row_mean = jnp.mean(values_in, -1, keepdims=True)
    centered = values_in - row_mean
    variance = jnp.mean(centered * centered, -1, keepdims=True)
    inv_std = lax.rsqrt(variance + NORM_EPS)
    return (centered * inv_std, inv_std)


def norm_back(grad_in, normed, inv_std, norm_gain):
    scaled = grad_in * norm_gain
    mean_scaled = jnp.mean(scaled, -1, keepdims=True)
    mean_mixed = jnp.mean(scaled * normed, -1, keepdims=True)
    return inv_std * (scaled - mean_scaled - normed * mean_mixed)


def across_rows(left_in, right_in):
    return lax.dot_general(left_in, right_in, (((0,), (0,)), ((), ())), preferred_element_type=F32)


def times_transposed(left_in, right_in):
    return lax.dot_general(left_in, right_in, (((1,), (1,)), ((), ())), preferred_element_type=F32)


def tensor_partners():
    here = lax.axis_index("tensor")
    core = lax.rem(here, 2)
    chip = here // 2
    return here, chip, core, 2 * chip + 1 - core, 2 * (1 - chip) + core


def send(source, landing, send_sem, recv_sem, target):
    return pltpu.make_async_remote_copy(
        src_ref=source,
        dst_ref=landing,
        send_sem=send_sem,
        recv_sem=recv_sem,
        device_id={"tensor": target},
        device_id_type=MESH,
    )


def side_copies(plan, sources, landings, send_sems, recv_sems):
    _, dp_others = others_along("dp")
    copies = []
    for i, (source, row, rows, column, width) in enumerate(plan):
        for k, target in enumerate(dp_others):
            first = pl.multiple_of(target * width, width) if column is None else column
            window = sources[source].at[pl.ds(row, rows), pl.ds(first, width)]
            copies.append(remote(window, landings[i].at[k], send_sems.at[i, k], recv_sems.at[i, k], {"dp": target}))
    return copies


def greet_tensor_and_dp(with_dp):
    _, _, _, partner, across = tensor_partners()
    targets = [{"tensor": partner}, {"tensor": across}]
    if with_dp:
        targets += [{"dp": other} for other in others_along("dp")[1]]
    greet_all(targets)


def side_shapes(plan, sources):
    n_far = lax.axis_size("dp") - 1
    return [jax.ShapeDtypeStruct((n_far, rows, width), sources[i].dtype) for i, _, rows, _, width in plan]


def side_sems(plan):
    return [pltpu.SemaphoreType.DMA((max(len(plan), 1), max(lax.axis_size("dp") - 1, 1)))] * 2


class Guest:
    def __init__(self, arrays, views, left, right, by_columns, far):
        self.arrays, self.views, self.left, self.right, self.by_columns = tuple(arrays), views, left, right, by_columns
        self.far_array, self.far_first = far
        self.far_shape = left if by_columns else right
        self.n_seq = lax.axis_size("seq")
        self.lanes = 256
        self.n_chunks = self.far_shape[1] // self.lanes
        self.n_far = lax.axis_size("dp") - 1
        self.tokens = left[0] // (self.n_far + 1)

    def out_shape(self):
        wide, across = self.left[1], self.right[1]
        shape = (self.n_seq * wide, across // self.n_seq) if self.by_columns else (wide, across)
        return jax.ShapeDtypeStruct(shape, BF16)

    def scratch(self):
        dma = pltpu.SemaphoreType.DMA
        far_sems = dma((max(self.n_far, 1), self.n_chunks))
        done = pltpu.VMEM(self.out_shape().shape, BF16)
        loads = dma((4 * (self.n_far + 1),))
        return [pltpu.VMEM(self.left, BF16), pltpu.VMEM(self.right, BF16), done, dma, loads, far_sems, far_sems]

    def loads(self, refs, scratch):
        pairs = self.views(refs, scratch[0], scratch[1])
        return [pltpu.make_async_copy(source, landing, scratch[4].at[i]) for i, (source, landing) in enumerate(pairs)]

    def far_copy(self, refs, scratch, k, c):
        _, dp_others = others_along("dp")
        side = scratch[0] if self.by_columns else scratch[1]
        source = refs[self.far_array].at[:, pl.ds(self.far_first + c * self.lanes, self.lanes)]
        landing = side.at[pl.ds((k + 1) * self.tokens, self.tokens), pl.ds(c * self.lanes, self.lanes)]
        return remote(source, landing, scratch[5].at[k, c], scratch[6].at[k, c], {"dp": dp_others[k]})

    def start(self, refs, scratch):
        for c in range(self.n_chunks):
            for k in range(self.n_far):
                self.far_copy(refs, scratch, k, c).start()
        for copy in self.loads(refs, scratch):
            copy.start()

    def run(self, refs, scratch, out_ref):
        left, right, done, done_sem = scratch[:4]
        for copy in self.loads(refs, scratch):
            copy.wait()
        at_once = 1 if self.by_columns else 2
        for c in range(0, self.n_chunks, at_once):
            for i in range(at_once):
                for k in range(self.n_far):
                    self.far_copy(refs, scratch, k, c + i).wait_recv()
            first, step = c * self.lanes, at_once * self.lanes
            a = left[:, first : first + step] if self.by_columns else left[...]
            b = right[...] if self.by_columns else right[:, first : first + step]
            block = lax.dot_general(a, b, (((0,), (0,)), ((), ())), preferred_element_type=F32).astype(BF16)
            if self.by_columns:
                piece, wide = block.shape[1] // self.n_seq, self.left[1]
                for s in range(self.n_seq):
                    done[s * wide + first : s * wide + first + step] = block[:, s * piece : (s + 1) * piece]
            else:
                done[:, first : first + step] = block
        copy = pltpu.make_async_copy(done, out_ref, done_sem)
        copy.start()
        for c in range(self.n_chunks):
            for k in range(self.n_far):
                self.far_copy(refs, scratch, k, c).wait_send()
        copy.wait()


def split_refs(refs, plan, n_sources, guest):
    n_guest = len(guest.arrays) if guest else 0
    sources, refs = refs[:n_sources], refs[n_sources:]
    guest_in, refs = refs[:n_guest], refs[n_guest:]
    o_ref, refs = refs[0], refs[1:]
    landings, refs = refs[: len(plan)], refs[len(plan) :]
    if not guest:
        return sources, guest_in, o_ref, landings, None, refs, None
    return sources, guest_in, o_ref, landings, refs[0], refs[1:-7], refs[-7:]


def reduce_kernel(transposed, plan, n_sources, guest, spread, a_ref, w_ref, *refs):
    if spread:
        spread_ref, ts, tr = refs[0], refs[-2], refs[-1]
        n_in = 1 + n_sources + len(guest.arrays)
        spread_all = refs[n_in + 1 + len(plan)]
        refs = refs[1 : n_in + 1 + len(plan)] + refs[n_in + 2 + len(plan) : -2]
    sources, guest_in, o_ref, landings, guest_out, refs, guest_scratch = split_refs(refs, plan, n_sources, guest)
    w_here, part, core_out, core_in, over_out, over_in, w_sem, cs, cr, xs, xr, side_s, side_r = refs
    n_blocks, width = core_out.shape[0], core_out.shape[-1]
    share = o_ref.shape[0]
    _, chip, core, partner, across = tensor_partners()

    def load(n):
        where = pl.ds(n * width, width)
        block = w_ref.at[where, :] if transposed else w_ref.at[:, where]
        return pltpu.make_async_copy(block, w_here.at[n], w_sem.at[n])

    def to_partner(n):
        return send(core_out.at[n], core_in.at[n], cs.at[n], cr.at[n], partner)

    def to_across(n):
        return send(over_out.at[n], over_in.at[n], xs.at[n], xr.at[n], across)

    for n in range(n_blocks):
        load(n).start()
    greet_tensor_and_dp(len(plan) > 0 or guest is not None)
    beside = side_copies(plan, sources, landings, side_s, side_r)
    for copy in beside:
        copy.start()
    if guest:
        guest.start(guest_in, guest_scratch)

    def multiply(n):
        load(n).wait()
        slot = lax.rem(n, 2)
        dims = (((1,), (1,)), ((), ())) if transposed else (((1,), (0,)), ((), ()))
        product = lax.dot_general(a_ref[...], w_here[n], dims, preferred_element_type=F32)
        part[slot] = product.reshape(4, share, width)
        core_out[n, 0] = part[slot, 1 - core].astype(BF16)
        core_out[n, 1] = part[slot, 3 - core].astype(BF16)
        to_partner(n).start()

    def pass_on(n):
        slot = lax.rem(n, 2)
        to_partner(n).wait_recv()
        over_out[n] = (part[slot, 2 * (1 - chip) + core] + core_in[n, 1 - chip].astype(F32)).astype(BF16)
        to_across(n).start()
        columns = pl.ds(pl.multiple_of(n * width, width), width)
        o_ref[:, columns] = part[slot, 2 * chip + core] + core_in[n, chip].astype(F32)

    def step(n, carry):
        multiply(n)

        @pl.when(n > 0)
        def _():
            pass_on(n - 1)

        return carry

    lax.fori_loop(0, n_blocks, step, 0)
    pass_on(n_blocks - 1)
    here, _, _, _, _ = tensor_partners()

    def spread_copy(source, owner, i, target):
        return remote(source, spread_all.at[owner], ts.at[i], tr.at[i], {"tensor": target})

    if spread:
        spread_copy(spread_ref, here, 0, across).start()
        spread_copy(spread_ref, here, 1, partner).start()
        own_copy = pltpu.make_async_copy(spread_ref, spread_all.at[here], ts.at[2])
        own_copy.start()

    def finish(n, carry):
        to_across(n).wait_recv()
        columns = pl.ds(pl.multiple_of(n * width, width), width)
        o_ref[:, columns] += over_in[n].astype(F32)
        to_across(n).wait_send()
        to_partner(n).wait_send()
        return carry

    lax.fori_loop(0, n_blocks, finish, 0)
    if spread:
        spread_copy(spread_ref, across, 0, across).wait_recv()
        spread_copy(spread_all.at[across], across, 3, partner).start()
        spread_copy(spread_ref, here, 0, across).wait_send()
        spread_copy(spread_ref, here, 1, partner).wait()
        spread_copy(spread_all.at[across], across, 3, partner).wait()
        own_copy.wait()
    for copy in beside:
        copy.wait()
    if guest:
        guest.run(guest_in, guest_scratch, guest_out)


def product_to_owners(name, number, a, w, transposed, sources=(), plan=(), guest=None, spread=None):
    tokens, depth = a.shape
    model_width = w.shape[0] if transposed else w.shape[1]
    share = tokens // 4
    width = model_width // 4
    n_blocks = 4
    w_block = (n_blocks, width, depth) if transposed else (n_blocks, depth, width)
    dma = pltpu.SemaphoreType.DMA((n_blocks,))
    extra = [] if spread is None else [spread]
    results = pl.pallas_call(
        functools.partial(reduce_kernel, transposed, plan, len(sources), guest, spread is not None),
        out_shape=[jax.ShapeDtypeStruct((share, model_width), F32)]
        + side_shapes(plan, sources)
        + [jax.ShapeDtypeStruct((4,) + e.shape, e.dtype) for e in extra]
        + guest_shape(guest),
        in_specs=[pl.BlockSpec(memory_space=pltpu.VMEM)] + anywhere(1 + len(extra) + len(sources)) + guest_specs(guest),
        out_specs=[pl.BlockSpec(memory_space=pltpu.VMEM)]
        + [pl.BlockSpec(memory_space=pltpu.HBM)] * len(extra)
        + side_specs(plan, guest),
        scratch_shapes=[
            pltpu.VMEM(w_block, BF16),
            pltpu.VMEM((2, 4, share, width), F32),
            pltpu.VMEM((n_blocks, 2, share, width), BF16),
            pltpu.VMEM((n_blocks, 2, share, width), BF16),
            pltpu.VMEM((n_blocks, share, width), BF16),
            pltpu.VMEM((n_blocks, share, width), BF16),
            dma,
            dma,
            dma,
            dma,
            dma,
        ]
        + side_sems(plan)
        + (guest.scratch() if guest else [])
        + [pltpu.SemaphoreType.DMA((4,))] * (2 * len(extra)),
        compiler_params=pltpu.CompilerParams(
            collective_id=number, has_side_effects=True, vmem_limit_bytes=52 * 1024 * 1024
        ),
        cost_estimate=estimate(25),
        name=name,
    )(a, w, *extra, *sources, *(guest.arrays if guest else ()))
    return results


def anywhere(count):
    return [pl.BlockSpec(memory_space=pl.ANY)] * count


def guest_specs(guest):
    return anywhere(len(guest.arrays)) if guest else []


def guest_shape(guest):
    return [guest.out_shape()] if guest else []


def side_specs(plan, guest):
    specs = [pl.BlockSpec(memory_space=pltpu.HBM)] * len(plan)
    return specs + ([pl.BlockSpec(memory_space=pltpu.HBM)] if guest else [])


def gather_kernel(plan, n_sources, guest, own_ref, *refs):
    sources, guest_in, o_ref, landings, guest_out, refs, guest_scratch = split_refs(refs, plan, n_sources, guest)
    cs, cr, xs, xr, fs, fr, side_s, side_r = refs
    n_chunks = cs.shape[0]
    share = own_ref.shape[0]
    rows = share // n_chunks
    here, _, _, partner, across = tensor_partners()

    def copy(source, owner, n, sems, target):
        where = pl.ds(n * rows, rows)
        return send(source.at[where], o_ref.at[owner, where], sems[0].at[n], sems[1].at[n], target)

    greet_tensor_and_dp(len(plan) > 0 or guest is not None)
    beside = side_copies(plan, sources, landings, side_s, side_r)
    for n in range(n_chunks):
        copy(own_ref, here, n, (xs, xr), across).start()
    for side in beside:
        side.start()
    for n in range(n_chunks):
        copy(own_ref, here, n, (cs, cr), partner).start()
    if guest:
        guest.start(guest_in, guest_scratch)
    o_ref[here] = own_ref[...]
    for n in range(n_chunks):
        copy(own_ref, here, n, (xs, xr), across).wait_recv()
        copy(o_ref.at[across], across, n, (fs, fr), partner).start()
    for n in range(n_chunks):
        copy(own_ref, here, n, (xs, xr), across).wait_send()
        copy(own_ref, here, n, (cs, cr), partner).wait()
        copy(o_ref.at[across], across, n, (fs, fr), partner).wait()
    for side in beside:
        side.wait()
    if guest:
        guest.run(guest_in, guest_scratch, guest_out)


def gather_shares(name, number, own, sources=(), plan=(), guest=None):
    share, width = own.shape
    dma = pltpu.SemaphoreType.DMA((4,))
    results = pl.pallas_call(
        functools.partial(gather_kernel, plan, len(sources), guest),
        out_shape=[jax.ShapeDtypeStruct((4, share, width), own.dtype)] + side_shapes(plan, sources) + guest_shape(guest),
        in_specs=[pl.BlockSpec(memory_space=pltpu.VMEM)] + anywhere(len(sources)) + guest_specs(guest),
        out_specs=[pl.BlockSpec(memory_space=pltpu.VMEM)] + side_specs(plan, guest),
        scratch_shapes=[dma] * 6 + side_sems(plan) + (guest.scratch() if guest else []),
        compiler_params=pltpu.CompilerParams(
            collective_id=number, has_side_effects=True, vmem_limit_bytes=32 * 1024 * 1024
        ),
        cost_estimate=estimate(20),
        name=name,
    )(own, *sources, *(guest.arrays if guest else ()))
    return (results[0].reshape(4 * share, width), *results[1:])


def front_kernel(
    grad_ref, kv_ref, o_ref, all_ref, cs, cr, xs, xr, fs, fr, zs, zr, kcs, kcr, kxs, kxr, kfs, kfr
):
    n_chunks = cs.shape[0]
    rows = grad_ref.shape[0] // n_chunks
    here, _, _, partner, across = tensor_partners()
    seq_me, seq_others = others_along("seq")
    greet_all([{"tensor": partner}, {"tensor": across}] + [{"seq": other} for other in seq_others])

    def copy(source, owner, n, sems, target):
        where = pl.ds(n * rows, rows)
        return send(source.at[where], o_ref.at[owner, where], sems[0].at[n], sems[1].at[n], target)

    def to_seq(source, owner, target):
        return remote(source, all_ref.at[owner, here], zs.at[target], zr.at[owner], {"seq": target})

    def keys(source, seq, owner, sems, target):
        return send(source, all_ref.at[seq, owner], sems[0].at[seq], sems[1].at[seq], target)

    for other in seq_others:
        to_seq(kv_ref, seq_me, other).start()
    keys(kv_ref, seq_me, here, (kxs, kxr), across).start()
    keys(kv_ref, seq_me, here, (kcs, kcr), partner).start()
    for n in range(n_chunks):
        copy(grad_ref, here, n, (xs, xr), across).start()
    for n in range(n_chunks):
        copy(grad_ref, here, n, (cs, cr), partner).start()
    all_ref[seq_me, here] = kv_ref[...]
    o_ref[here] = grad_ref[...]
    for other in seq_others:
        remote(kv_ref, all_ref.at[other, here], zs.at[other], zr.at[other], {"seq": other}).wait_recv()
        keys(all_ref.at[other, here], other, here, (kxs, kxr), across).start()
        keys(all_ref.at[other, here], other, here, (kcs, kcr), partner).start()
    keys(kv_ref, seq_me, across, (kxs, kxr), across).wait_recv()
    keys(all_ref.at[seq_me, across], seq_me, across, (kfs, kfr), partner).start()
    for n in range(n_chunks):
        copy(grad_ref, here, n, (xs, xr), across).wait_recv()
        copy(o_ref.at[across], across, n, (fs, fr), partner).start()
    for other in seq_others:
        keys(kv_ref, other, across, (kxs, kxr), across).wait_recv()
        keys(all_ref.at[other, across], other, across, (kfs, kfr), partner).start()
    for n in range(n_chunks):
        copy(grad_ref, here, n, (xs, xr), across).wait_send()
        copy(grad_ref, here, n, (cs, cr), partner).wait()
        copy(o_ref.at[across], across, n, (fs, fr), partner).wait()
    for other in seq_others:
        to_seq(kv_ref, seq_me, other).wait_send()
    for seq in [seq_me] + seq_others:
        keys(kv_ref, seq, here, (kxs, kxr), across).wait_send()
        keys(kv_ref, seq, here, (kcs, kcr), partner).wait()
        keys(all_ref.at[seq, across], seq, across, (kfs, kfr), partner).wait()


def front(number, grad_own, kv_own):
    n_seq = lax.axis_size("seq")
    share, width = grad_own.shape
    dma = pltpu.SemaphoreType.DMA
    vmem = pl.BlockSpec(memory_space=pltpu.VMEM)
    grads, kv_all = pl.pallas_call(
        front_kernel,
        out_shape=(
            jax.ShapeDtypeStruct((4, share, width), BF16),
            jax.ShapeDtypeStruct((n_seq, 4) + kv_own.shape, BF16),
        ),
        in_specs=[vmem] * 2,
        out_specs=(vmem,) * 2,
        scratch_shapes=[dma((4,))] * 6 + [dma((n_seq,))] * 8,
        compiler_params=pltpu.CompilerParams(
            collective_id=number, has_side_effects=True, vmem_limit_bytes=16 * 1024 * 1024
        ),
        cost_estimate=estimate(30),
        name="front",
    )(grad_own, kv_own)
    return grads.reshape(4 * share, width), kv_all


def remote(source, landing, send_sem, recv_sem, target):
    return pltpu.make_async_remote_copy(
        src_ref=source,
        dst_ref=landing,
        send_sem=send_sem,
        recv_sem=recv_sem,
        device_id=target,
        device_id_type=MESH,
    )


def greet_all(targets):
    barrier = pltpu.get_barrier_semaphore()
    for target in targets:
        pl.semaphore_signal(barrier, inc=1, device_id=target, device_id_type=MESH)
    pl.semaphore_wait(barrier, len(targets))


def others_along(axis):
    size = lax.axis_size(axis)
    me = lax.axis_index(axis)
    return me, [lax.rem(me + k, size) for k in range(1, size)]


def kv_kernel(plan, n_sources, guest, g_ref, *refs):
    sources, guest_in, o_ref, landings, guest_out, refs, guest_scratch = split_refs(refs, plan, n_sources, guest)
    core_in, over_out, over_in, seq_out, seq_in, own = refs[:6]
    cs, cr, xs, xr, zs, zr, gs, gr, side_s, side_r = refs[6:]
    here, chip, core, partner, across = tensor_partners()
    seq_me, seq_others = others_along("seq")
    greet_all(
        [{"tensor": partner}, {"tensor": across}]
        + [{"seq": other} for other in seq_others]
        + [{"dp": other} for other in others_along("dp")[1]]
    )
    beside = side_copies(plan, sources, landings, side_s, side_r)
    for copy in beside:
        copy.start()
    guest.start(guest_in, guest_scratch)

    def to_partner(j):
        return remote(g_ref.at[2 * j + 1 - core], core_in.at[j], cs.at[j], cr.at[j], {"tensor": partner})

    to_partner(1 - chip).start()
    to_partner(chip).start()
    to_partner(1 - chip).wait()
    over_out[...] = (g_ref[2 * (1 - chip) + core].astype(F32) + core_in[1 - chip].astype(F32)).astype(BF16)
    to_across = remote(over_out, over_in, xs.at[0], xr.at[0], {"tensor": across})
    to_across.start()
    to_partner(chip).wait()
    to_across.wait()
    seq_out[...] = (
        g_ref[2 * chip + core].astype(F32) + core_in[chip].astype(F32) + over_in[...].astype(F32)
    ).astype(BF16)

    def to_seq(target):
        return remote(seq_out.at[target], seq_in.at[seq_me], zs.at[target], zr.at[seq_me], {"seq": target})

    for other in seq_others:
        to_seq(other).start()
    total = seq_out[seq_me].astype(F32)
    for other in seq_others:
        remote(seq_out.at[other], seq_in.at[other], zs.at[other], zr.at[other], {"seq": other}).wait_recv()
        total = total + seq_in[other].astype(F32)
    own[...] = total.astype(BF16)
    o_ref[here] = own[...]
    x_copy = remote(own, o_ref.at[here], gs.at[0], gr.at[0], {"tensor": across})
    c_copy = remote(own, o_ref.at[here], gs.at[1], gr.at[1], {"tensor": partner})
    x_copy.start()
    c_copy.start()
    x_copy.wait_recv()
    f_copy = remote(o_ref.at[across], o_ref.at[across], gs.at[2], gr.at[2], {"tensor": partner})
    f_copy.start()
    x_copy.wait_send()
    c_copy.wait()
    f_copy.wait()
    for other in seq_others:
        to_seq(other).wait_send()
    guest.run(guest_in, guest_scratch, guest_out)
    for copy in beside:
        copy.wait()


def sum_grad_kv(number, parts, sources, plan, guest):
    _, n_seq, share, width = parts.shape
    dma = pltpu.SemaphoreType.DMA
    vmem = pl.BlockSpec(memory_space=pltpu.VMEM)
    results = pl.pallas_call(
        functools.partial(kv_kernel, plan, len(sources), guest),
        out_shape=[
            jax.ShapeDtypeStruct((4, share, width), BF16),
        ]
        + side_shapes(plan, sources)
        + guest_shape(guest),
        in_specs=[vmem] + anywhere(len(sources)) + guest_specs(guest),
        out_specs=[vmem] + side_specs(plan, guest),
        scratch_shapes=[
            pltpu.VMEM((2, n_seq, share, width), BF16),
            pltpu.VMEM((n_seq, share, width), BF16),
            pltpu.VMEM((n_seq, share, width), BF16),
            pltpu.VMEM((n_seq, share, width), BF16),
            pltpu.VMEM((n_seq, share, width), BF16),
            pltpu.VMEM((share, width), BF16),
            dma((2,)),
            dma((2,)),
            dma((1,)),
            dma((1,)),
            dma((n_seq,)),
            dma((n_seq,)),
            dma((3,)),
            dma((3,)),
        ]
        + side_sems(plan)
        + guest.scratch(),
        compiler_params=pltpu.CompilerParams(
            collective_id=number, has_side_effects=True, vmem_limit_bytes=40 * 1024 * 1024
        ),
        cost_estimate=estimate(30),
        name="sum_grad_kv",
    )(parts, *sources, *guest.arrays)
    return (results[0].reshape(4 * share, width), *results[1:])


def estimate(microseconds):
    return pl.CostEstimate(flops=int(microseconds * 1e6), bytes_accessed=0, transcendentals=0)


def attention_kernel(len_ref, q_ref, kv_ref, o_ref, lse_ref, scores):
    share = o_ref.shape[0] // 4
    n_rows = len_ref.shape[0]
    tile = share // n_rows
    block = 4 * tile
    head = kv_ref.shape[-1] // 2
    heads = q_ref.shape[1] // head
    lanes = heads * tile
    seq_me = lax.axis_index("seq")

    def one_tile(t, carry):
        quarter = t // n_rows
        row = t - quarter * n_rows
        length = len_ref[row]
        first = seq_me * block + quarter * tile
        where = pl.ds(pl.multiple_of(t * tile, tile), tile)
        own_rows = pl.ds(pl.multiple_of(row * tile, tile), tile)

        @pl.when(first >= length)
        def _():
            o_ref[where, :] = jnp.zeros((tile, heads * head), BF16)
            lse_ref[t] = jnp.zeros((1, lanes), F32)

        @pl.when(first < length)
        def _():
            queries = q_ref[where, :]
            stacked = jnp.concatenate([queries[:, h * head : (h + 1) * head] for h in range(heads)], 0)
            n_blocks = jnp.minimum(seq_me + 1, (length + block - 1) // block)
            place = first + lax.rem(lax.broadcasted_iota(jnp.int32, (1, lanes), 1), tile)
            limit = jnp.minimum(place + 1, length)
            key_index = lax.broadcasted_iota(jnp.int32, (block, lanes), 0)

            def score(b, highest):
                keys = kv_ref[b, :, own_rows, :head].reshape(block, head)
                s = lax.dot_general(keys, stacked, (((1,), (1,)), ((), ())), preferred_element_type=F32)
                s = jnp.where(key_index < limit - b * block, s, -1e30)
                scores[b] = s
                return jnp.maximum(highest, jnp.max(s, 0, keepdims=True))

            highest = lax.fori_loop(0, n_blocks, score, jnp.full((1, lanes), -1e30, F32))

            def mix(b, both):
                total, mixed = both
                values = kv_ref[b, :, own_rows, head:].reshape(block, head)
                p = jnp.exp(scores[b] - highest)
                total = total + jnp.sum(p, 0, keepdims=True)
                mixed = mixed + lax.dot_general(
                    values, p.astype(BF16), (((0,), (0,)), ((), ())), preferred_element_type=F32
                )
                return total, mixed

            total, mixed = lax.fori_loop(
                0, n_blocks, mix, (jnp.zeros((1, lanes), F32), jnp.zeros((head, lanes), F32))
            )
            lse_ref[t] = highest + jnp.log(total)
            back = jnp.transpose(mixed / total)
            o_ref[where, :] = jnp.concatenate(
                [back[h * tile : (h + 1) * tile] for h in range(heads)], 1
            ).astype(BF16)

        return carry

    lax.fori_loop(0, 4 * n_rows, one_tile, 0)


def attention(lengths, queries, kv_all):
    tokens, width = queries.shape
    n_rows = lengths.shape[0]
    n_seq, kv_width = kv_all.shape[0], kv_all.shape[-1]
    tile = tokens // (4 * n_rows)
    lanes = width // (kv_width // 2) * tile
    return pl.pallas_call(
        attention_kernel,
        out_shape=(
            jax.ShapeDtypeStruct((tokens, width), BF16),
            jax.ShapeDtypeStruct((4 * n_rows, 1, lanes), F32),
        ),
        in_specs=[pl.BlockSpec(memory_space=pltpu.SMEM)] + [pl.BlockSpec(memory_space=pltpu.VMEM)] * 2,
        out_specs=(pl.BlockSpec(memory_space=pltpu.VMEM),) * 2,
        scratch_shapes=[pltpu.VMEM((n_seq, 4 * tile, lanes), F32)],
        compiler_params=pltpu.CompilerParams(vmem_limit_bytes=24 * 1024 * 1024),
        cost_estimate=estimate(10),
        name="attention",
    )(lengths, queries, kv_all)


def attention_back_kernel(len_ref, q_ref, do_ref, kv_ref, lse_ref, dq_ref, dkv_ref, probs, grads, total, keys_t):
    share = dq_ref.shape[0] // 4
    n_rows = len_ref.shape[0]
    tile = share // n_rows
    block = 4 * tile
    head = kv_ref.shape[-1] // 2
    heads = q_ref.shape[1] // head
    lanes = heads * tile
    n_seq = total.shape[0]
    seq_me = lax.axis_index("seq")

    def one_row(row, carry):
        length = len_ref[row]
        n_blocks = jnp.minimum(seq_me + 1, (length + block - 1) // block)
        total[...] = jnp.zeros_like(total)
        own_rows = pl.ds(pl.multiple_of(row * tile, tile), tile)
        for b in range(n_seq):
            keys_t[b] = jnp.transpose(kv_ref[b, :, own_rows, :head].reshape(block, head).astype(F32)).astype(BF16)

        def one_tile(quarter, carry):
            t = quarter * n_rows + row
            first = seq_me * block + quarter * tile
            where = pl.ds(pl.multiple_of(t * tile, tile), tile)

            @pl.when(first >= length)
            def _():
                dq_ref[where, :] = jnp.zeros((tile, heads * head), BF16)

            @pl.when(first < length)
            def _():
                def stack(ref):
                    rows = ref[where, :]
                    return jnp.concatenate([rows[:, h * head : (h + 1) * head] for h in range(heads)], 0)

                stacked = stack(q_ref)
                outer = stack(do_ref)
                lse = lse_ref[t]
                place = first + lax.rem(lax.broadcasted_iota(jnp.int32, (1, lanes), 1), tile)
                limit = jnp.minimum(place + 1, length)
                key_index = lax.broadcasted_iota(jnp.int32, (block, lanes), 0)

                def score(b, inner):
                    keys = kv_ref[b, :, own_rows, :head].reshape(block, head)
                    values = kv_ref[b, :, own_rows, head:].reshape(block, head)
                    s = lax.dot_general(keys, stacked, (((1,), (1,)), ((), ())), preferred_element_type=F32)
                    p = jnp.where(key_index < limit - b * block, jnp.exp(s - lse), 0.0)
                    g = lax.dot_general(values, outer, (((1,), (1,)), ((), ())), preferred_element_type=F32)
                    probs[b] = p
                    grads[b] = g
                    total[b, :, head:] += jnp.dot(p.astype(BF16), outer, preferred_element_type=F32)
                    return inner + jnp.sum(p * g, 0, keepdims=True)

                inner = lax.fori_loop(0, n_blocks, score, jnp.zeros((1, lanes), F32))

                def back(b, dq):
                    ds = (probs[b] * (grads[b] - inner)).astype(BF16)
                    total[b, :, :head] += jnp.dot(ds, stacked, preferred_element_type=F32)
                    return dq + jnp.dot(keys_t[b], ds, preferred_element_type=F32)

                dq = jnp.transpose(lax.fori_loop(0, n_blocks, back, jnp.zeros((head, lanes), F32)))
                dq_ref[where, :] = jnp.concatenate(
                    [dq[h * tile : (h + 1) * tile] for h in range(heads)], 1
                ).astype(BF16)

            return carry

        lax.fori_loop(0, 4, one_tile, 0)
        for quarter in range(4):
            for b in range(n_seq):
                dkv_ref[quarter, b, own_rows, :] = total[b, quarter * tile : (quarter + 1) * tile, :].astype(BF16)
        return carry

    lax.fori_loop(0, n_rows, one_row, 0)


def attention_back(lengths, queries, grad_mixed, kv_all, lse):
    tokens, width = queries.shape
    n_rows = lengths.shape[0]
    n_seq, kv_width = kv_all.shape[0], kv_all.shape[-1]
    tile = tokens // (4 * n_rows)
    lanes = width // (kv_width // 2) * tile
    block = 4 * tile
    return pl.pallas_call(
        attention_back_kernel,
        out_shape=(
            jax.ShapeDtypeStruct((tokens, width), BF16),
            jax.ShapeDtypeStruct((4, n_seq, tokens // 4, kv_width), BF16),
        ),
        in_specs=[pl.BlockSpec(memory_space=pltpu.SMEM)] + [pl.BlockSpec(memory_space=pltpu.VMEM)] * 4,
        out_specs=(pl.BlockSpec(memory_space=pltpu.VMEM),) * 2,
        scratch_shapes=[
            pltpu.VMEM((n_seq, block, lanes), F32),
            pltpu.VMEM((n_seq, block, lanes), F32),
            pltpu.VMEM((n_seq, block, kv_width), F32),
            pltpu.VMEM((n_seq, kv_width // 2, block), BF16),
        ],
        compiler_params=pltpu.CompilerParams(vmem_limit_bytes=32 * 1024 * 1024),
        cost_estimate=estimate(25),
        name="attention_back",
    )(lengths, queries, grad_mixed, kv_all, lse)


def last_kernel(n_all, n_local, q_ref, kv_ref, out_ref, _, *refs):
    small_refs, refs = refs[: n_all + n_local], refs[n_all + n_local :]
    q_sum, kv_sum, out_sum, small = refs[:4]
    packed, dp_in, near_out, near_in, far_out, far_in, total, small_core, small_x, small_dp, small_seq = refs[4:15]
    ys, yr, ns, nr, fs, fr, ss, sr = refs[15:]
    shared = small_core.shape[0]
    _, _, _, partner, across = tensor_partners()
    rows = q_ref.shape[2]
    kv_rows, kv_width = kv_ref.shape[3:]
    per_line = q_ref.shape[3] // kv_width
    lines = kv_rows // per_line
    here = lax.axis_index("tensor")
    dp_me, dp_others = others_along("dp")
    seq_me = lax.axis_index("seq")
    beside = seq_me + 1 - 2 * lax.rem(seq_me, 2)
    far = seq_me + 2 - 4 * (seq_me // 2)
    opposite = 3 - seq_me
    greet_all(
        [{"tensor": partner}, {"tensor": across}]
        + [{"dp": other} for other in dp_others]
        + [{"seq": beside}, {"seq": far}]
    )
    small[...] = jnp.zeros_like(small)
    for i, ref in enumerate(small_refs):
        row = i if i < n_all else shared + i - n_all
        small[row : row + 1, : ref.shape[1]] = ref[...]
    head_rows = pl.ds(0, shared)
    small_to_partner = remote(small.at[head_rows], small_core, ss.at[0], sr.at[0], {"tensor": partner})
    small_to_across = remote(small.at[head_rows], small_x, ss.at[1], sr.at[1], {"tensor": across})
    small_to_beside = remote(small, small_seq.at[0], ss.at[2], sr.at[2], {"seq": beside})
    small_to_far = remote(small, small_seq.at[1], ss.at[3], sr.at[3], {"seq": far})

    def small_to_dp(k):
        return remote(small, small_dp.at[k], ss.at[4 + k], sr.at[4 + k], {"dp": dp_others[k]})

    small_to_partner.start()

    def to_dp(k, b):
        return remote(packed.at[dp_others[k], b], dp_in.at[k, b], ys.at[k, b], yr.at[k, b], {"dp": dp_others[k]})

    def pack(d, b):
        packed[d, b, :rows] = q_ref[d, b]
        packed[d, b, rows : 2 * rows] = out_ref[d, b]
        for i in range(per_line):
            packed[d, b, 2 * rows :, i * kv_width : (i + 1) * kv_width] = kv_ref[
                d, b, here, i * lines : (i + 1) * lines
            ]

    order = (beside, opposite, far, seq_me)
    for i, b in enumerate(order):
        for k, d in enumerate(dp_others):
            pack(d, b)
            to_dp(k, b).start()
        if i == 0:
            small_to_partner.wait()
            small[:shared] += small_core[...]
            small_to_across.start()
            small_to_across.wait()
            small[:shared] += small_x[...]
            for k in range(len(dp_others)):
                small_to_dp(k).start()
    for b in order:
        pack(dp_me, b)

    def summed(b):
        value = packed[dp_me, b].astype(F32)
        for k in range(len(dp_others)):
            to_dp(k, b).wait_recv()
            value = value + dp_in[k, b].astype(F32)
        return value

    def to_beside(i):
        return remote(near_out.at[i], near_in.at[i], ns.at[i], nr.at[i], {"seq": beside})

    near_out[0] = summed(beside).astype(BF16)
    to_beside(0).start()
    for k in range(len(dp_others)):
        small_to_dp(k).wait()
    for k in range(len(dp_others)):
        small[...] += small_dp[k]
    small_to_beside.start()
    near_out[1] = summed(opposite).astype(BF16)
    to_beside(1).start()
    total[...] = summed(far)
    small_to_beside.wait()
    small[...] += small_seq[0]
    small_to_far.start()
    to_beside(1).wait_recv()
    far_out[...] = (total[...] + near_in[1].astype(F32)).astype(BF16)
    to_far = remote(far_out, far_in, fs.at[0], fr.at[0], {"seq": far})
    to_far.start()
    total[...] = summed(seq_me)
    to_beside(0).wait_recv()
    total[...] += near_in[0].astype(F32)
    to_far.wait_recv()
    total[...] += far_in[...].astype(F32)
    small_to_far.wait()
    small[...] += small_seq[1]
    q_sum[...] = total[:rows]
    out_sum[...] = jnp.transpose(total[rows : 2 * rows])
    for i in range(per_line):
        kv_sum[i * lines : (i + 1) * lines] = total[2 * rows :, i * kv_width : (i + 1) * kv_width]
    for b in order:
        for k in range(len(dp_others)):
            to_dp(k, b).wait_send()
    to_beside(0).wait_send()
    to_beside(1).wait_send()
    to_far.wait_send()


def sum_last(number, q_part, kv_part, out_part, earlier, summed_all, summed_local):
    n_dp, n_seq, rows, width = q_part.shape
    kv_rows, kv_width = kv_part.shape[3:]
    block = (2 * rows + kv_rows * kv_width // width, width)
    n_far = n_dp - 1
    dma = pltpu.SemaphoreType.DMA
    vmem = pl.BlockSpec(memory_space=pltpu.VMEM)
    lanes = summed_all[0].shape[1]
    return pl.pallas_call(
        functools.partial(last_kernel, len(summed_all), len(summed_local)),
        out_shape=(
            jax.ShapeDtypeStruct((rows, width), F32),
            jax.ShapeDtypeStruct((kv_rows, kv_width), F32),
            jax.ShapeDtypeStruct((width, rows), F32),
            jax.ShapeDtypeStruct((16, lanes), F32),
        ),
        in_specs=[vmem] * 3 + anywhere(1) + [vmem] * (len(summed_all) + len(summed_local)),
        out_specs=(vmem,) * 4,
        scratch_shapes=[
            pltpu.VMEM((n_dp, n_seq) + block, BF16),
            pltpu.VMEM((n_far, n_seq) + block, BF16),
            pltpu.VMEM((2,) + block, BF16),
            pltpu.VMEM((2,) + block, BF16),
            pltpu.VMEM(block, BF16),
            pltpu.VMEM(block, BF16),
            pltpu.VMEM(block, F32),
            pltpu.VMEM((8, lanes), F32),
            pltpu.VMEM((8, lanes), F32),
            pltpu.VMEM((n_far, 16, lanes), F32),
            pltpu.VMEM((2, 16, lanes), F32),
            dma((n_far, n_seq)),
            dma((n_far, n_seq)),
            dma((2,)),
            dma((2,)),
            dma((1,)),
            dma((1,)),
            dma((4 + n_far,)),
            dma((4 + n_far,)),
        ],
        compiler_params=pltpu.CompilerParams(
            collective_id=number, has_side_effects=True, vmem_limit_bytes=48 * 1024 * 1024
        ),
        cost_estimate=estimate(70),
        name="sum_last",
    )(q_part, kv_part, out_part, earlier, *summed_all, *summed_local)


def shards(
    layer_input,
    lengths,
    cotangent,
    ln1_gain,
    ln1_bias,
    w_query,
    b_query,
    w_kv,
    b_value,
    w_out,
    b_out,
    ln2_gain,
    ln2_bias,
    w_up,
    b_up,
    w_down,
    b_down,
):
    n_rows, seq_len, model_width = layer_input.shape
    n_tensor = lax.axis_size("tensor")
    n_dp = lax.axis_size("dp")
    n_seq = lax.axis_size("seq")
    share_len = seq_len // n_tensor
    tensor_index = lax.axis_index("tensor")
    seq_index = lax.axis_index("seq")
    head_size = w_kv.shape[1] // 2
    num_heads = w_query.shape[1] // head_size
    q_scale = 1.0 / math.sqrt(head_size)
    n_tok = n_rows * seq_len
    n_own = n_rows * share_len

    def by_share(values_in):
        return jnp.moveaxis(values_in.reshape((n_rows, n_tensor, share_len) + values_in.shape[2:]), 1, 0)

    def own_share(values_in):
        return lax.dynamic_index_in_dim(values_in.reshape((n_tensor, n_own) + values_in.shape[1:]), tensor_index, 0, False)

    positions = seq_index * seq_len + jnp.arange(seq_len, dtype=jnp.int32)
    is_valid = (positions[None, :] < lengths[:, None]).astype(F32)
    valid_own = own_share(by_share(is_valid).reshape(n_tok))[:, None]
    grad_y_own = cotangent.reshape(n_own, model_width).astype(F32) * valid_own
    x_float = lax.optimization_barrier(by_share(layer_input).reshape(n_tok, model_width)).astype(F32)
    normed_x1, inv_one = normalize(x_float)
    flat_one = (normed_x1 * ln1_gain + ln1_bias).astype(BF16)
    kv_bias = jnp.concatenate([jnp.zeros((head_size,), F32), b_value.astype(F32)])
    kv_own = (jnp.dot(own_share(flat_one), w_kv, preferred_element_type=F32) + kv_bias).astype(BF16)
    queries = ((jnp.dot(flat_one, w_query, preferred_element_type=F32) + b_query) * q_scale).astype(BF16)
    grad_y_low, kv_all = front(0, grad_y_own.astype(BF16), kv_own)

    half_width = model_width // n_dp
    hidden = w_up.shape[1]
    dp_me = lax.axis_index("dp")

    first_rows = n_tok * 5 // 128 * 16
    mixed_heads, log_total = attention(lengths, queries, kv_all)
    attn_own, grad_y_far_a = product_to_owners(
        "attn_out", 1, mixed_heads, w_out, False, (grad_y_low,), ((0, 0, first_rows, None, half_width),)
    )
    x_own = own_share(x_float)
    resid_own = x_own + (attn_own + b_out)
    normed_x2, inv_two = normalize(resid_own)
    normed_two = (normed_x2 * ln2_gain + ln2_bias).astype(BF16)
    flat_two, grad_y_far_b, two_far_own = gather_shares(
        "gather_norm_two",
        2,
        normed_two,
        (grad_y_low, normed_two),
        ((0, first_rows, n_tok - first_rows, None, half_width), (1, 0, n_own, None, half_width)),
    )
    pre_act = jnp.dot(flat_two, w_up, preferred_element_type=F32) + b_up
    activated, gelu_pull = jax.vjp(lambda inner_in: jax.nn.gelu(inner_in, approximate=True), pre_act)
    act_low = activated.astype(BF16)
    grad_act = times_transposed(grad_y_low, w_down)
    grad_pre = gelu_pull(grad_act)[0].astype(BF16)

    def mine(ref):
        return ref.at[:, pl.ds(pl.multiple_of(lax.axis_index("dp") * half_width, half_width), half_width)]

    def tokens_of(ref, k, first=0, rows=n_tok):
        return ref.at[pl.ds((k + 1) * n_tok + first, rows)]

    group = hidden * 3 // 8
    half_hidden = hidden // 2

    def part_down(first, width):
        def views(refs, left, right):
            act, grads, grads_far_a, grads_far_b = refs
            pairs = [(act.at[:, pl.ds(first, width)], tokens_of(left, -1)), (mine(grads), tokens_of(right, -1))]
            for k in range(n_dp - 1):
                pairs.append((grads_far_a.at[k], tokens_of(right, k, 0, first_rows)))
                pairs.append((grads_far_b.at[k], tokens_of(right, k, first_rows, n_tok - first_rows)))
            return pairs

        arrays = (act_low, grad_y_low, grad_y_far_a, grad_y_far_b)
        return Guest(arrays, views, (n_dp * n_tok, width), (n_dp * n_tok, half_width), True, (0, first))

    def part_up(first, width):
        def views(refs, left, right):
            two, far_two, pre = refs
            pairs = [(mine(two), tokens_of(left, -1)), (pre.at[:, pl.ds(first, width)], tokens_of(right, -1))]
            for k in range(n_dp - 1):
                pairs.append((far_two.at[:, pl.ds(k * half_width, half_width)], tokens_of(left, k)))
            return pairs

        arrays = (flat_two, two_far, grad_pre)
        return Guest(arrays, views, (n_dp * n_tok, half_width), (n_dp * n_tok, width), False, (2, first))

    def over_seq(values_in):
        return lax.psum_scatter(values_in, "seq", scatter_dimension=0, tiled=True)

    grad_n2, down_a = product_to_owners("grad_norm_two", 3, grad_pre, w_up, True, guest=part_down(0, group))
    down_a = over_seq(down_a)
    grad_resid = grad_y_own + norm_back(grad_n2, normed_x2, inv_two, ln2_gain)
    grad_resid_low = grad_resid.astype(BF16)
    flat_resid, down_b = gather_shares("gather_grad_resid", 4, grad_resid_low, guest=part_down(group, group))
    down_b = over_seq(down_b)
    grad_mixed = times_transposed(flat_resid, w_out).astype(BF16)
    flat_query, grad_kv = attention_back(lengths, queries, grad_mixed, kv_all, log_total)
    two_swapped = jnp.swapaxes(two_far_own, 0, 1).reshape(n_own, -1)
    grad_n1, two_far, down_c = product_to_owners(
        "grad_norm_one",
        6,
        flat_query,
        w_query,
        True,
        (down_a,),
        guest=part_down(2 * group, hidden - 2 * group),
        spread=two_swapped,
    )
    down_c = over_seq(down_c)
    grad_n1 = grad_n1 * q_scale
    two_far = two_far.reshape(n_tok, (n_dp - 1) * half_width)
    flat_kv, up_a = sum_grad_kv(7, grad_kv, (down_b,), (), part_up(0, half_hidden))
    up_a = over_seq(up_a)
    mlp_raw, up_b = product_to_owners(
        "mlp_out", 5, act_low, w_down, False, (flat_kv, down_c), guest=part_up(half_hidden, half_hidden)
    )
    up_b = over_seq(up_b)
    mlp_own = mlp_raw + b_down
    g_w_down = jnp.concatenate([down_a, down_b, down_c], 0).astype(F32)
    g_w_up = jnp.concatenate([up_a, up_b], 1).astype(F32)

    def by_owner(values_in, *between):
        return values_in.astype(BF16).reshape((n_dp, n_seq) + between + (-1, values_in.shape[1]))

    q_part = by_owner(across_rows(flat_one, flat_query) * q_scale)
    kv_part = by_owner(across_rows(flat_one, flat_kv), n_tensor)
    out_part = by_owner(across_rows(flat_resid, mixed_heads))
    y_own = (valid_own * (resid_own + mlp_own)).astype(BF16).reshape(n_rows, share_len, model_width)

    own_kv = own_share(flat_kv)
    grad_n1 = grad_n1 + times_transposed(own_kv, w_kv)
    normed_x1_own = own_share(normed_x1)
    x_grad_own = grad_resid + norm_back(grad_n1, normed_x1_own, own_share(inv_one), ln1_gain)
    x_grad_own = x_grad_own.reshape(n_rows, share_len, model_width)
    def token_sum(values_in):
        return jnp.sum(values_in.astype(F32), axis=0, keepdims=True)

    over_all = [
        token_sum(grad_n1 * normed_x1_own),
        token_sum(grad_n1),
        token_sum(grad_n2 * normed_x2),
        token_sum(grad_n2),
        token_sum(grad_resid_low),
        token_sum(grad_y_own),
        token_sum(own_kv[:, head_size:]),
    ]
    over_local = [token_sum(grad_pre), token_sum(flat_query) * q_scale]
    g_w_query, g_w_kv, g_w_out, small = sum_last(9, q_part, kv_part, out_part, up_a, over_all, over_local)
    owners = n_dp * n_seq
    owner = dp_me * n_seq + seq_index
    last_owner = owner * n_tensor + tensor_index

    def owned(values_in, index, count):
        width = values_in.shape[-1] // count
        return lax.dynamic_slice_in_dim(values_in, index * width, width, values_in.ndim - 1)

    query_out = owned(small[9, : num_heads * head_size].reshape(num_heads, head_size), owner, owners)
    up_out = owned(small[8].reshape(-1, 128), owner, owners)
    small_out = owned(small[:6], last_owner, owners * n_tensor)
    value_out = owned(small[6, :head_size], last_owner, owners * n_tensor)
    return (
        y_own,
        x_grad_own,
        g_w_query,
        query_out,
        g_w_kv,
        value_out,
        g_w_out,
        g_w_up,
        up_out,
        g_w_down,
        small_out,
    )


def solution(mesh):
    placed = (
        P("dp", "seq", None),
        P("dp"),
        P("dp", ("seq", "tensor"), None),
        P(),
        P(),
        P(None, "tensor"),
        P("tensor"),
        P(),
        P(),
        P("tensor", None),
        P(),
        P(),
        P(),
        P(None, "tensor"),
        P("tensor"),
        P("tensor", None),
        P(),
    )
    return jax.shard_map(
        shards,
        mesh=mesh,
        in_specs=placed,
        out_specs=(
            P("dp", ("seq", "tensor"), None),
            P("dp", ("seq", "tensor"), None),
            P(("dp", "seq"), "tensor"),
            P("tensor", ("dp", "seq")),
            P(("dp", "seq", "tensor"), None),
            P(("dp", "seq", "tensor")),
            P("tensor", ("dp", "seq")),
            P(("dp", "seq"), "tensor"),
            P("tensor", ("dp", "seq")),
            P("tensor", ("dp", "seq")),
            P(None, ("dp", "seq", "tensor")),
        ),
        check_vma=False,
    )
```

```python
import functools
import math

import jax
import jax.numpy as jnp
from jax import lax
from jax.experimental import pallas as pl
from jax.experimental.pallas import tpu as pltpu
from jax.sharding import PartitionSpec as P

NORM_EPS = 1e-05
BF16 = jnp.bfloat16
F32 = jnp.float32
MESH = pl.DeviceIdType.MESH


def normalize(values_in):
    row_mean = jnp.mean(values_in, -1, keepdims=True)
    centered = values_in - row_mean
    variance = jnp.mean(centered * centered, -1, keepdims=True)
    inv_std = lax.rsqrt(variance + NORM_EPS)
    return (centered * inv_std, inv_std)


def norm_back(grad_in, normed, inv_std, norm_gain):
    scaled = grad_in * norm_gain
    mean_scaled = jnp.mean(scaled, -1, keepdims=True)
    mean_mixed = jnp.mean(scaled * normed, -1, keepdims=True)
    return inv_std * (scaled - mean_scaled - normed * mean_mixed)


def across_rows(left_in, right_in):
    return lax.dot_general(left_in, right_in, (((0,), (0,)), ((), ())), preferred_element_type=F32)


def times_transposed(left_in, right_in):
    return lax.dot_general(left_in, right_in, (((1,), (1,)), ((), ())), preferred_element_type=F32)


def tensor_partners():
    here = lax.axis_index("tensor")
    core = lax.rem(here, 2)
    chip = here // 2
    return here, chip, core, 2 * chip + 1 - core, 2 * (1 - chip) + core


def send(source, landing, send_sem, recv_sem, target):
    return pltpu.make_async_remote_copy(
        src_ref=source,
        dst_ref=landing,
        send_sem=send_sem,
        recv_sem=recv_sem,
        device_id={"tensor": target},
        device_id_type=MESH,
    )


def side_copies(plan, sources, landings, send_sems, recv_sems):
    _, dp_others = others_along("dp")
    copies = []
    for i, (source, row, rows, column, width) in enumerate(plan):
        for k, target in enumerate(dp_others):
            first = pl.multiple_of(target * width, width) if column is None else column
            window = sources[source].at[pl.ds(row, rows), pl.ds(first, width)]
            copies.append(remote(window, landings[i].at[k], send_sems.at[i, k], recv_sems.at[i, k], {"dp": target}))
    return copies


def greet_tensor_and_dp(with_dp):
    _, _, _, partner, across = tensor_partners()
    targets = [{"tensor": partner}, {"tensor": across}]
    if with_dp:
        targets += [{"dp": other} for other in others_along("dp")[1]]
    greet_all(targets)


def side_shapes(plan, sources):
    n_far = lax.axis_size("dp") - 1
    return [jax.ShapeDtypeStruct((n_far, rows, width), sources[i].dtype) for i, _, rows, _, width in plan]


def side_sems(plan):
    return [pltpu.SemaphoreType.DMA((max(len(plan), 1), max(lax.axis_size("dp") - 1, 1)))] * 2


class Guest:
    def __init__(self, arrays, views, left, right, by_columns, far):
        self.arrays, self.views, self.left, self.right, self.by_columns = tuple(arrays), views, left, right, by_columns
        self.far_array, self.far_first = far
        self.far_shape = left if by_columns else right
        self.n_seq = lax.axis_size("seq")
        self.lanes = 256
        self.n_chunks = self.far_shape[1] // self.lanes
        self.n_far = lax.axis_size("dp") - 1
        self.tokens = left[0] // (self.n_far + 1)

    def out_shape(self):
        wide, across = self.left[1], self.right[1]
        shape = (self.n_seq * wide, across // self.n_seq) if self.by_columns else (wide, across)
        return jax.ShapeDtypeStruct(shape, BF16)

    def scratch(self):
        dma = pltpu.SemaphoreType.DMA
        far_sems = dma((max(self.n_far, 1), self.n_chunks))
        done = pltpu.VMEM(self.out_shape().shape, BF16)
        loads = dma((4 * (self.n_far + 1),))
        return [pltpu.VMEM(self.left, BF16), pltpu.VMEM(self.right, BF16), done, dma, loads, far_sems, far_sems]

    def loads(self, refs, scratch):
        pairs = self.views(refs, scratch[0], scratch[1])
        return [pltpu.make_async_copy(source, landing, scratch[4].at[i]) for i, (source, landing) in enumerate(pairs)]

    def far_copy(self, refs, scratch, k, c):
        _, dp_others = others_along("dp")
        side = scratch[0] if self.by_columns else scratch[1]
        source = refs[self.far_array].at[:, pl.ds(self.far_first + c * self.lanes, self.lanes)]
        landing = side.at[pl.ds((k + 1) * self.tokens, self.tokens), pl.ds(c * self.lanes, self.lanes)]
        return remote(source, landing, scratch[5].at[k, c], scratch[6].at[k, c], {"dp": dp_others[k]})

    def start(self, refs, scratch):
        for c in range(self.n_chunks):
            for k in range(self.n_far):
                self.far_copy(refs, scratch, k, c).start()
        for copy in self.loads(refs, scratch):
            copy.start()

    def run(self, refs, scratch, out_ref):
        left, right, done, done_sem = scratch[:4]
        for copy in self.loads(refs, scratch):
            copy.wait()
        at_once = 1 if self.by_columns else 2
        for c in range(0, self.n_chunks, at_once):
            for i in range(at_once):
                for k in range(self.n_far):
                    self.far_copy(refs, scratch, k, c + i).wait_recv()
            first, step = c * self.lanes, at_once * self.lanes
            a = left[:, first : first + step] if self.by_columns else left[...]
            b = right[...] if self.by_columns else right[:, first : first + step]
            block = lax.dot_general(a, b, (((0,), (0,)), ((), ())), preferred_element_type=F32).astype(BF16)
            if self.by_columns:
                piece, wide = block.shape[1] // self.n_seq, self.left[1]
                for s in range(self.n_seq):
                    done[s * wide + first : s * wide + first + step] = block[:, s * piece : (s + 1) * piece]
            else:
                done[:, first : first + step] = block
        copy = pltpu.make_async_copy(done, out_ref, done_sem)
        copy.start()
        for c in range(self.n_chunks):
            for k in range(self.n_far):
                self.far_copy(refs, scratch, k, c).wait_send()
        copy.wait()


def split_refs(refs, plan, n_sources, guest):
    n_guest = len(guest.arrays) if guest else 0
    sources, refs = refs[:n_sources], refs[n_sources:]
    guest_in, refs = refs[:n_guest], refs[n_guest:]
    o_ref, refs = refs[0], refs[1:]
    landings, refs = refs[: len(plan)], refs[len(plan) :]
    if not guest:
        return sources, guest_in, o_ref, landings, None, refs, None
    return sources, guest_in, o_ref, landings, refs[0], refs[1:-7], refs[-7:]


def reduce_kernel(transposed, plan, n_sources, guest, spread, a_ref, w_ref, *refs):
    if spread:
        spread_ref, ts, tr = refs[0], refs[-2], refs[-1]
        n_in = 1 + n_sources + len(guest.arrays)
        spread_all = refs[n_in + 1 + len(plan)]
        refs = refs[1 : n_in + 1 + len(plan)] + refs[n_in + 2 + len(plan) : -2]
    sources, guest_in, o_ref, landings, guest_out, refs, guest_scratch = split_refs(refs, plan, n_sources, guest)
    w_here, part, core_out, core_in, over_out, over_in, w_sem, cs, cr, xs, xr, side_s, side_r = refs
    n_blocks, width = core_out.shape[0], core_out.shape[-1]
    share = o_ref.shape[0]
    _, chip, core, partner, across = tensor_partners()

    def load(n):
        where = pl.ds(n * width, width)
        block = w_ref.at[where, :] if transposed else w_ref.at[:, where]
        return pltpu.make_async_copy(block, w_here.at[n], w_sem.at[n])

    def to_partner(n):
        return send(core_out.at[n], core_in.at[n], cs.at[n], cr.at[n], partner)

    def to_across(n):
        return send(over_out.at[n], over_in.at[n], xs.at[n], xr.at[n], across)

    for n in range(n_blocks):
        load(n).start()
    greet_tensor_and_dp(len(plan) > 0 or guest is not None)
    beside = side_copies(plan, sources, landings, side_s, side_r)
    for copy in beside:
        copy.start()
    if guest:
        guest.start(guest_in, guest_scratch)

    def multiply(n):
        load(n).wait()
        slot = lax.rem(n, 2)
        dims = (((1,), (1,)), ((), ())) if transposed else (((1,), (0,)), ((), ()))
        product = lax.dot_general(a_ref[...], w_here[n], dims, preferred_element_type=F32)
        part[slot] = product.reshape(4, share, width)
        core_out[n, 0] = part[slot, 1 - core].astype(BF16)
        core_out[n, 1] = part[slot, 3 - core].astype(BF16)
        to_partner(n).start()

    def pass_on(n):
        slot = lax.rem(n, 2)
        to_partner(n).wait_recv()
        over_out[n] = (part[slot, 2 * (1 - chip) + core] + core_in[n, 1 - chip].astype(F32)).astype(BF16)
        to_across(n).start()
        columns = pl.ds(pl.multiple_of(n * width, width), width)
        o_ref[:, columns] = part[slot, 2 * chip + core] + core_in[n, chip].astype(F32)

    def step(n, carry):
        multiply(n)

        @pl.when(n > 0)
        def _():
            pass_on(n - 1)

        return carry

    lax.fori_loop(0, n_blocks, step, 0)
    pass_on(n_blocks - 1)
    here, _, _, _, _ = tensor_partners()

    def spread_copy(source, owner, i, target):
        return remote(source, spread_all.at[owner], ts.at[i], tr.at[i], {"tensor": target})

    if spread:
        spread_copy(spread_ref, here, 0, across).start()
        spread_copy(spread_ref, here, 1, partner).start()
        own_copy = pltpu.make_async_copy(spread_ref, spread_all.at[here], ts.at[2])
        own_copy.start()

    def finish(n, carry):
        to_across(n).wait_recv()
        columns = pl.ds(pl.multiple_of(n * width, width), width)
        o_ref[:, columns] += over_in[n].astype(F32)
        to_across(n).wait_send()
        to_partner(n).wait_send()
        return carry

    lax.fori_loop(0, n_blocks, finish, 0)
    if spread:
        spread_copy(spread_ref, across, 0, across).wait_recv()
        spread_copy(spread_all.at[across], across, 3, partner).start()
        spread_copy(spread_ref, here, 0, across).wait_send()
        spread_copy(spread_ref, here, 1, partner).wait()
        spread_copy(spread_all.at[across], across, 3, partner).wait()
        own_copy.wait()
    for copy in beside:
        copy.wait()
    if guest:
        guest.run(guest_in, guest_scratch, guest_out)


def product_to_owners(name, number, a, w, transposed, sources=(), plan=(), guest=None, spread=None):
    tokens, depth = a.shape
    model_width = w.shape[0] if transposed else w.shape[1]
    share = tokens // 4
    width = model_width // 4
    n_blocks = 4
    w_block = (n_blocks, width, depth) if transposed else (n_blocks, depth, width)
    dma = pltpu.SemaphoreType.DMA((n_blocks,))
    extra = [] if spread is None else [spread]
    results = pl.pallas_call(
        functools.partial(reduce_kernel, transposed, plan, len(sources), guest, spread is not None),
        out_shape=[jax.ShapeDtypeStruct((share, model_width), F32)]
        + side_shapes(plan, sources)
        + [jax.ShapeDtypeStruct((4,) + e.shape, e.dtype) for e in extra]
        + guest_shape(guest),
        in_specs=[pl.BlockSpec(memory_space=pltpu.VMEM)] + anywhere(1 + len(extra) + len(sources)) + guest_specs(guest),
        out_specs=[pl.BlockSpec(memory_space=pltpu.VMEM)]
        + [pl.BlockSpec(memory_space=pltpu.HBM)] * len(extra)
        + side_specs(plan, guest),
        scratch_shapes=[
            pltpu.VMEM(w_block, BF16),
            pltpu.VMEM((2, 4, share, width), F32),
            pltpu.VMEM((n_blocks, 2, share, width), BF16),
            pltpu.VMEM((n_blocks, 2, share, width), BF16),
            pltpu.VMEM((n_blocks, share, width), BF16),
            pltpu.VMEM((n_blocks, share, width), BF16),
            dma,
            dma,
            dma,
            dma,
            dma,
        ]
        + side_sems(plan)
        + (guest.scratch() if guest else [])
        + [pltpu.SemaphoreType.DMA((4,))] * (2 * len(extra)),
        compiler_params=pltpu.CompilerParams(
            collective_id=number, has_side_effects=True, vmem_limit_bytes=52 * 1024 * 1024
        ),
        cost_estimate=estimate(25),
        name=name,
    )(a, w, *extra, *sources, *(guest.arrays if guest else ()))
    return results


def anywhere(count):
    return [pl.BlockSpec(memory_space=pl.ANY)] * count


def guest_specs(guest):
    return anywhere(len(guest.arrays)) if guest else []


def guest_shape(guest):
    return [guest.out_shape()] if guest else []


def side_specs(plan, guest):
    specs = [pl.BlockSpec(memory_space=pltpu.HBM)] * len(plan)
    return specs + ([pl.BlockSpec(memory_space=pltpu.HBM)] if guest else [])


def gather_kernel(plan, n_sources, guest, own_ref, *refs):
    sources, guest_in, o_ref, landings, guest_out, refs, guest_scratch = split_refs(refs, plan, n_sources, guest)
    cs, cr, xs, xr, fs, fr, side_s, side_r = refs
    n_chunks = cs.shape[0]
    share = own_ref.shape[0]
    rows = share // n_chunks
    here, _, _, partner, across = tensor_partners()

    def copy(source, owner, n, sems, target):
        where = pl.ds(n * rows, rows)
        return send(source.at[where], o_ref.at[owner, where], sems[0].at[n], sems[1].at[n], target)

    greet_tensor_and_dp(len(plan) > 0 or guest is not None)
    beside = side_copies(plan, sources, landings, side_s, side_r)
    for n in range(n_chunks):
        copy(own_ref, here, n, (xs, xr), across).start()
    for side in beside:
        side.start()
    for n in range(n_chunks):
        copy(own_ref, here, n, (cs, cr), partner).start()
    if guest:
        guest.start(guest_in, guest_scratch)
    o_ref[here] = own_ref[...]
    for n in range(n_chunks):
        copy(own_ref, here, n, (xs, xr), across).wait_recv()
        copy(o_ref.at[across], across, n, (fs, fr), partner).start()
    for n in range(n_chunks):
        copy(own_ref, here, n, (xs, xr), across).wait_send()
        copy(own_ref, here, n, (cs, cr), partner).wait()
        copy(o_ref.at[across], across, n, (fs, fr), partner).wait()
    for side in beside:
        side.wait()
    if guest:
        guest.run(guest_in, guest_scratch, guest_out)


def gather_shares(name, number, own, sources=(), plan=(), guest=None):
    share, width = own.shape
    dma = pltpu.SemaphoreType.DMA((4,))
    results = pl.pallas_call(
        functools.partial(gather_kernel, plan, len(sources), guest),
        out_shape=[jax.ShapeDtypeStruct((4, share, width), own.dtype)] + side_shapes(plan, sources) + guest_shape(guest),
        in_specs=[pl.BlockSpec(memory_space=pltpu.VMEM)] + anywhere(len(sources)) + guest_specs(guest),
        out_specs=[pl.BlockSpec(memory_space=pltpu.VMEM)] + side_specs(plan, guest),
        scratch_shapes=[dma] * 6 + side_sems(plan) + (guest.scratch() if guest else []),
        compiler_params=pltpu.CompilerParams(
            collective_id=number, has_side_effects=True, vmem_limit_bytes=32 * 1024 * 1024
        ),
        cost_estimate=estimate(20),
        name=name,
    )(own, *sources, *(guest.arrays if guest else ()))
    return (results[0].reshape(4 * share, width), *results[1:])


def front_kernel(
    grad_ref, kv_ref, o_ref, all_ref, cs, cr, xs, xr, fs, fr, zs, zr, kcs, kcr, kxs, kxr, kfs, kfr
):
    n_chunks = cs.shape[0]
    rows = grad_ref.shape[0] // n_chunks
    here, _, _, partner, across = tensor_partners()
    seq_me, seq_others = others_along("seq")
    greet_all([{"tensor": partner}, {"tensor": across}] + [{"seq": other} for other in seq_others])

    def copy(source, owner, n, sems, target):
        where = pl.ds(n * rows, rows)
        return send(source.at[where], o_ref.at[owner, where], sems[0].at[n], sems[1].at[n], target)

    def to_seq(source, owner, target):
        return remote(source, all_ref.at[owner, here], zs.at[target], zr.at[owner], {"seq": target})

    def keys(source, seq, owner, sems, target):
        return send(source, all_ref.at[seq, owner], sems[0].at[seq], sems[1].at[seq], target)

    for other in seq_others:
        to_seq(kv_ref, seq_me, other).start()
    keys(kv_ref, seq_me, here, (kxs, kxr), across).start()
    keys(kv_ref, seq_me, here, (kcs, kcr), partner).start()
    for n in range(n_chunks):
        copy(grad_ref, here, n, (xs, xr), across).start()
    for n in range(n_chunks):
        copy(grad_ref, here, n, (cs, cr), partner).start()
    all_ref[seq_me, here] = kv_ref[...]
    o_ref[here] = grad_ref[...]
    for other in seq_others:
        remote(kv_ref, all_ref.at[other, here], zs.at[other], zr.at[other], {"seq": other}).wait_recv()
        keys(all_ref.at[other, here], other, here, (kxs, kxr), across).start()
        keys(all_ref.at[other, here], other, here, (kcs, kcr), partner).start()
    keys(kv_ref, seq_me, across, (kxs, kxr), across).wait_recv()
    keys(all_ref.at[seq_me, across], seq_me, across, (kfs, kfr), partner).start()
    for n in range(n_chunks):
        copy(grad_ref, here, n, (xs, xr), across).wait_recv()
        copy(o_ref.at[across], across, n, (fs, fr), partner).start()
    for other in seq_others:
        keys(kv_ref, other, across, (kxs, kxr), across).wait_recv()
        keys(all_ref.at[other, across], other, across, (kfs, kfr), partner).start()
    for n in range(n_chunks):
        copy(grad_ref, here, n, (xs, xr), across).wait_send()
        copy(grad_ref, here, n, (cs, cr), partner).wait()
        copy(o_ref.at[across], across, n, (fs, fr), partner).wait()
    for other in seq_others:
        to_seq(kv_ref, seq_me, other).wait_send()
    for seq in [seq_me] + seq_others:
        keys(kv_ref, seq, here, (kxs, kxr), across).wait_send()
        keys(kv_ref, seq, here, (kcs, kcr), partner).wait()
        keys(all_ref.at[seq, across], seq, across, (kfs, kfr), partner).wait()


def front(number, grad_own, kv_own):
    n_seq = lax.axis_size("seq")
    share, width = grad_own.shape
    dma = pltpu.SemaphoreType.DMA
    vmem = pl.BlockSpec(memory_space=pltpu.VMEM)
    grads, kv_all = pl.pallas_call(
        front_kernel,
        out_shape=(
            jax.ShapeDtypeStruct((4, share, width), BF16),
            jax.ShapeDtypeStruct((n_seq, 4) + kv_own.shape, BF16),
        ),
        in_specs=[vmem] * 2,
        out_specs=(vmem,) * 2,
        scratch_shapes=[dma((4,))] * 6 + [dma((n_seq,))] * 8,
        compiler_params=pltpu.CompilerParams(
            collective_id=number, has_side_effects=True, vmem_limit_bytes=16 * 1024 * 1024
        ),
        cost_estimate=estimate(30),
        name="front",
    )(grad_own, kv_own)
    return grads.reshape(4 * share, width), kv_all


def remote(source, landing, send_sem, recv_sem, target):
    return pltpu.make_async_remote_copy(
        src_ref=source,
        dst_ref=landing,
        send_sem=send_sem,
        recv_sem=recv_sem,
        device_id=target,
        device_id_type=MESH,
    )


def greet_all(targets):
    barrier = pltpu.get_barrier_semaphore()
    for target in targets:
        pl.semaphore_signal(barrier, inc=1, device_id=target, device_id_type=MESH)
    pl.semaphore_wait(barrier, len(targets))


def others_along(axis):
    size = lax.axis_size(axis)
    me = lax.axis_index(axis)
    return me, [lax.rem(me + k, size) for k in range(1, size)]


def kv_kernel(plan, n_sources, guest, g_ref, *refs):
    sources, guest_in, o_ref, landings, guest_out, refs, guest_scratch = split_refs(refs, plan, n_sources, guest)
    core_in, over_out, over_in, seq_out, seq_in, own = refs[:6]
    cs, cr, xs, xr, zs, zr, gs, gr, side_s, side_r = refs[6:]
    here, chip, core, partner, across = tensor_partners()
    seq_me, seq_others = others_along("seq")
    greet_all(
        [{"tensor": partner}, {"tensor": across}]
        + [{"seq": other} for other in seq_others]
        + [{"dp": other} for other in others_along("dp")[1]]
    )
    beside = side_copies(plan, sources, landings, side_s, side_r)
    for copy in beside:
        copy.start()
    guest.start(guest_in, guest_scratch)

    def to_partner(j):
        return remote(g_ref.at[2 * j + 1 - core], core_in.at[j], cs.at[j], cr.at[j], {"tensor": partner})

    to_partner(1 - chip).start()
    to_partner(chip).start()
    to_partner(1 - chip).wait()
    over_out[...] = (g_ref[2 * (1 - chip) + core].astype(F32) + core_in[1 - chip].astype(F32)).astype(BF16)
    to_across = remote(over_out, over_in, xs.at[0], xr.at[0], {"tensor": across})
    to_across.start()
    to_partner(chip).wait()
    to_across.wait()
    seq_out[...] = (
        g_ref[2 * chip + core].astype(F32) + core_in[chip].astype(F32) + over_in[...].astype(F32)
    ).astype(BF16)

    def to_seq(target):
        return remote(seq_out.at[target], seq_in.at[seq_me], zs.at[target], zr.at[seq_me], {"seq": target})

    for other in seq_others:
        to_seq(other).start()
    total = seq_out[seq_me].astype(F32)
    for other in seq_others:
        remote(seq_out.at[other], seq_in.at[other], zs.at[other], zr.at[other], {"seq": other}).wait_recv()
        total = total + seq_in[other].astype(F32)
    own[...] = total.astype(BF16)
    o_ref[here] = own[...]
    x_copy = remote(own, o_ref.at[here], gs.at[0], gr.at[0], {"tensor": across})
    c_copy = remote(own, o_ref.at[here], gs.at[1], gr.at[1], {"tensor": partner})
    x_copy.start()
    c_copy.start()
    x_copy.wait_recv()
    f_copy = remote(o_ref.at[across], o_ref.at[across], gs.at[2], gr.at[2], {"tensor": partner})
    f_copy.start()
    x_copy.wait_send()
    c_copy.wait()
    f_copy.wait()
    for other in seq_others:
        to_seq(other).wait_send()
    guest.run(guest_in, guest_scratch, guest_out)
    for copy in beside:
        copy.wait()


def sum_grad_kv(number, parts, sources, plan, guest):
    _, n_seq, share, width = parts.shape
    dma = pltpu.SemaphoreType.DMA
    vmem = pl.BlockSpec(memory_space=pltpu.VMEM)
    results = pl.pallas_call(
        functools.partial(kv_kernel, plan, len(sources), guest),
        out_shape=[
            jax.ShapeDtypeStruct((4, share, width), BF16),
        ]
        + side_shapes(plan, sources)
        + guest_shape(guest),
        in_specs=[vmem] + anywhere(len(sources)) + guest_specs(guest),
        out_specs=[vmem] + side_specs(plan, guest),
        scratch_shapes=[
            pltpu.VMEM((2, n_seq, share, width), BF16),
            pltpu.VMEM((n_seq, share, width), BF16),
            pltpu.VMEM((n_seq, share, width), BF16),
            pltpu.VMEM((n_seq, share, width), BF16),
            pltpu.VMEM((n_seq, share, width), BF16),
            pltpu.VMEM((share, width), BF16),
            dma((2,)),
            dma((2,)),
            dma((1,)),
            dma((1,)),
            dma((n_seq,)),
            dma((n_seq,)),
            dma((3,)),
            dma((3,)),
        ]
        + side_sems(plan)
        + guest.scratch(),
        compiler_params=pltpu.CompilerParams(
            collective_id=number, has_side_effects=True, vmem_limit_bytes=40 * 1024 * 1024
        ),
        cost_estimate=estimate(30),
        name="sum_grad_kv",
    )(parts, *sources, *guest.arrays)
    return (results[0].reshape(4 * share, width), *results[1:])


def estimate(microseconds):
    return pl.CostEstimate(flops=int(microseconds * 1e6), bytes_accessed=0, transcendentals=0)


def attention_kernel(len_ref, q_ref, kv_ref, o_ref, lse_ref, scores):
    share = o_ref.shape[0] // 4
    n_rows = len_ref.shape[0]
    tile = share // n_rows
    block = 4 * tile
    head = kv_ref.shape[-1] // 2
    heads = q_ref.shape[1] // head
    lanes = heads * tile
    seq_me = lax.axis_index("seq")

    def one_tile(t, carry):
        quarter = t // n_rows
        row = t - quarter * n_rows
        length = len_ref[row]
        first = seq_me * block + quarter * tile
        where = pl.ds(pl.multiple_of(t * tile, tile), tile)
        own_rows = pl.ds(pl.multiple_of(row * tile, tile), tile)

        @pl.when(first >= length)
        def _():
            o_ref[where, :] = jnp.zeros((tile, heads * head), BF16)
            lse_ref[t] = jnp.zeros((1, lanes), F32)

        @pl.when(first < length)
        def _():
            queries = q_ref[where, :]
            stacked = jnp.concatenate([queries[:, h * head : (h + 1) * head] for h in range(heads)], 0)
            n_blocks = jnp.minimum(seq_me + 1, (length + block - 1) // block)
            place = first + lax.rem(lax.broadcasted_iota(jnp.int32, (1, lanes), 1), tile)
            limit = jnp.minimum(place + 1, length)
            key_index = lax.broadcasted_iota(jnp.int32, (block, lanes), 0)

            def score(b, highest):
                keys = kv_ref[b, :, own_rows, :head].reshape(block, head)
                s = lax.dot_general(keys, stacked, (((1,), (1,)), ((), ())), preferred_element_type=F32)
                s = jnp.where(key_index < limit - b * block, s, -1e30)
                scores[b] = s
                return jnp.maximum(highest, jnp.max(s, 0, keepdims=True))

            highest = lax.fori_loop(0, n_blocks, score, jnp.full((1, lanes), -1e30, F32))

            def mix(b, both):
                total, mixed = both
                values = kv_ref[b, :, own_rows, head:].reshape(block, head)
                p = jnp.exp(scores[b] - highest)
                total = total + jnp.sum(p, 0, keepdims=True)
                mixed = mixed + lax.dot_general(
                    values, p.astype(BF16), (((0,), (0,)), ((), ())), preferred_element_type=F32
                )
                return total, mixed

            total, mixed = lax.fori_loop(
                0, n_blocks, mix, (jnp.zeros((1, lanes), F32), jnp.zeros((head, lanes), F32))
            )
            lse_ref[t] = highest + jnp.log(total)
            back = jnp.transpose(mixed / total)
            o_ref[where, :] = jnp.concatenate(
                [back[h * tile : (h + 1) * tile] for h in range(heads)], 1
            ).astype(BF16)

        return carry

    lax.fori_loop(0, 4 * n_rows, one_tile, 0)


def attention(lengths, queries, kv_all):
    tokens, width = queries.shape
    n_rows = lengths.shape[0]
    n_seq, kv_width = kv_all.shape[0], kv_all.shape[-1]
    tile = tokens // (4 * n_rows)
    lanes = width // (kv_width // 2) * tile
    return pl.pallas_call(
        attention_kernel,
        out_shape=(
            jax.ShapeDtypeStruct((tokens, width), BF16),
            jax.ShapeDtypeStruct((4 * n_rows, 1, lanes), F32),
        ),
        in_specs=[pl.BlockSpec(memory_space=pltpu.SMEM)] + [pl.BlockSpec(memory_space=pltpu.VMEM)] * 2,
        out_specs=(pl.BlockSpec(memory_space=pltpu.VMEM),) * 2,
        scratch_shapes=[pltpu.VMEM((n_seq, 4 * tile, lanes), F32)],
        compiler_params=pltpu.CompilerParams(vmem_limit_bytes=24 * 1024 * 1024),
        cost_estimate=estimate(10),
        name="attention",
    )(lengths, queries, kv_all)


def attention_back_kernel(len_ref, q_ref, do_ref, kv_ref, lse_ref, dq_ref, dkv_ref, probs, grads, total, keys_t):
    share = dq_ref.shape[0] // 4
    n_rows = len_ref.shape[0]
    tile = share // n_rows
    block = 4 * tile
    head = kv_ref.shape[-1] // 2
    heads = q_ref.shape[1] // head
    lanes = heads * tile
    n_seq = total.shape[0]
    seq_me = lax.axis_index("seq")

    def one_row(row, carry):
        length = len_ref[row]
        n_blocks = jnp.minimum(seq_me + 1, (length + block - 1) // block)
        total[...] = jnp.zeros_like(total)
        own_rows = pl.ds(pl.multiple_of(row * tile, tile), tile)
        for b in range(n_seq):
            keys_t[b] = jnp.transpose(kv_ref[b, :, own_rows, :head].reshape(block, head).astype(F32)).astype(BF16)

        def one_tile(quarter, carry):
            t = quarter * n_rows + row
            first = seq_me * block + quarter * tile
            where = pl.ds(pl.multiple_of(t * tile, tile), tile)

            @pl.when(first >= length)
            def _():
                dq_ref[where, :] = jnp.zeros((tile, heads * head), BF16)

            @pl.when(first < length)
            def _():
                def stack(ref):
                    rows = ref[where, :]
                    return jnp.concatenate([rows[:, h * head : (h + 1) * head] for h in range(heads)], 0)

                stacked = stack(q_ref)
                outer = stack(do_ref)
                lse = lse_ref[t]
                place = first + lax.rem(lax.broadcasted_iota(jnp.int32, (1, lanes), 1), tile)
                limit = jnp.minimum(place + 1, length)
                key_index = lax.broadcasted_iota(jnp.int32, (block, lanes), 0)

                def score(b, inner):
                    keys = kv_ref[b, :, own_rows, :head].reshape(block, head)
                    values = kv_ref[b, :, own_rows, head:].reshape(block, head)
                    s = lax.dot_general(keys, stacked, (((1,), (1,)), ((), ())), preferred_element_type=F32)
                    p = jnp.where(key_index < limit - b * block, jnp.exp(s - lse), 0.0)
                    g = lax.dot_general(values, outer, (((1,), (1,)), ((), ())), preferred_element_type=F32)
                    probs[b] = p
                    grads[b] = g
                    total[b, :, head:] += jnp.dot(p.astype(BF16), outer, preferred_element_type=F32)
                    return inner + jnp.sum(p * g, 0, keepdims=True)

                inner = lax.fori_loop(0, n_blocks, score, jnp.zeros((1, lanes), F32))

                def back(b, dq):
                    ds = (probs[b] * (grads[b] - inner)).astype(BF16)
                    total[b, :, :head] += jnp.dot(ds, stacked, preferred_element_type=F32)
                    return dq + jnp.dot(keys_t[b], ds, preferred_element_type=F32)

                dq = jnp.transpose(lax.fori_loop(0, n_blocks, back, jnp.zeros((head, lanes), F32)))
                dq_ref[where, :] = jnp.concatenate(
                    [dq[h * tile : (h + 1) * tile] for h in range(heads)], 1
                ).astype(BF16)

            return carry

        lax.fori_loop(0, 4, one_tile, 0)
        for quarter in range(4):
            for b in range(n_seq):
                dkv_ref[quarter, b, own_rows, :] = total[b, quarter * tile : (quarter + 1) * tile, :].astype(BF16)
        return carry

    lax.fori_loop(0, n_rows, one_row, 0)


def attention_back(lengths, queries, grad_mixed, kv_all, lse):
    tokens, width = queries.shape
    n_rows = lengths.shape[0]
    n_seq, kv_width = kv_all.shape[0], kv_all.shape[-1]
    tile = tokens // (4 * n_rows)
    lanes = width // (kv_width // 2) * tile
    block = 4 * tile
    return pl.pallas_call(
        attention_back_kernel,
        out_shape=(
            jax.ShapeDtypeStruct((tokens, width), BF16),
            jax.ShapeDtypeStruct((4, n_seq, tokens // 4, kv_width), BF16),
        ),
        in_specs=[pl.BlockSpec(memory_space=pltpu.SMEM)] + [pl.BlockSpec(memory_space=pltpu.VMEM)] * 4,
        out_specs=(pl.BlockSpec(memory_space=pltpu.VMEM),) * 2,
        scratch_shapes=[
            pltpu.VMEM((n_seq, block, lanes), F32),
            pltpu.VMEM((n_seq, block, lanes), F32),
            pltpu.VMEM((n_seq, block, kv_width), F32),
            pltpu.VMEM((n_seq, kv_width // 2, block), BF16),
        ],
        compiler_params=pltpu.CompilerParams(vmem_limit_bytes=32 * 1024 * 1024),
        cost_estimate=estimate(25),
        name="attention_back",
    )(lengths, queries, grad_mixed, kv_all, lse)


def last_kernel(n_all, n_local, q_ref, kv_ref, out_ref, _, *refs):
    small_refs, refs = refs[: n_all + n_local], refs[n_all + n_local :]
    q_sum, kv_sum, out_sum, small = refs[:4]
    packed, dp_in, near_out, near_in, far_out, far_in, total, small_core, small_x, small_dp, small_seq = refs[4:15]
    ys, yr, ns, nr, fs, fr, ss, sr = refs[15:]
    shared = small_core.shape[0]
    _, _, _, partner, across = tensor_partners()
    rows = q_ref.shape[2]
    kv_rows, kv_width = kv_ref.shape[3:]
    per_line = q_ref.shape[3] // kv_width
    lines = kv_rows // per_line
    here = lax.axis_index("tensor")
    dp_me, dp_others = others_along("dp")
    seq_me = lax.axis_index("seq")
    beside = seq_me + 1 - 2 * lax.rem(seq_me, 2)
    far = seq_me + 2 - 4 * (seq_me // 2)
    opposite = 3 - seq_me
    greet_all(
        [{"tensor": partner}, {"tensor": across}]
        + [{"dp": other} for other in dp_others]
        + [{"seq": beside}, {"seq": far}]
    )
    small[...] = jnp.zeros_like(small)
    for i, ref in enumerate(small_refs):
        row = i if i < n_all else shared + i - n_all
        small[row : row + 1, : ref.shape[1]] = ref[...]
    head_rows = pl.ds(0, shared)
    small_to_partner = remote(small.at[head_rows], small_core, ss.at[0], sr.at[0], {"tensor": partner})
    small_to_across = remote(small.at[head_rows], small_x, ss.at[1], sr.at[1], {"tensor": across})
    small_to_beside = remote(small, small_seq.at[0], ss.at[2], sr.at[2], {"seq": beside})
    small_to_far = remote(small, small_seq.at[1], ss.at[3], sr.at[3], {"seq": far})

    def small_to_dp(k):
        return remote(small, small_dp.at[k], ss.at[4 + k], sr.at[4 + k], {"dp": dp_others[k]})

    small_to_partner.start()

    def to_dp(k, b):
        return remote(packed.at[dp_others[k], b], dp_in.at[k, b], ys.at[k, b], yr.at[k, b], {"dp": dp_others[k]})

    def pack(d, b):
        packed[d, b, :rows] = q_ref[d, b]
        packed[d, b, rows : 2 * rows] = out_ref[d, b]
        for i in range(per_line):
            packed[d, b, 2 * rows :, i * kv_width : (i + 1) * kv_width] = kv_ref[
                d, b, here, i * lines : (i + 1) * lines
            ]

    order = (opposite, far, beside, seq_me)
    for i, b in enumerate(order):
        for k, d in enumerate(dp_others):
            pack(d, b)
            to_dp(k, b).start()
        if i == 0:
            small_to_partner.wait()
            small[:shared] += small_core[...]
            small_to_across.start()
            small_to_across.wait()
            small[:shared] += small_x[...]
            for k in range(len(dp_others)):
                small_to_dp(k).start()
    for b in order:
        pack(dp_me, b)

    def summed(b):
        value = packed[dp_me, b].astype(F32)
        for k in range(len(dp_others)):
            to_dp(k, b).wait_recv()
            value = value + dp_in[k, b].astype(F32)
        return value

    def to_beside(i):
        return remote(near_out.at[i], near_in.at[i], ns.at[i], nr.at[i], {"seq": beside})

    near_out[1] = summed(opposite).astype(BF16)
    to_beside(1).start()
    for k in range(len(dp_others)):
        small_to_dp(k).wait()
    for k in range(len(dp_others)):
        small[...] += small_dp[k]
    small_to_beside.start()
    total[...] = summed(far)
    to_beside(1).wait_recv()
    far_out[...] = (total[...] + near_in[1].astype(F32)).astype(BF16)
    to_far = remote(far_out, far_in, fs.at[0], fr.at[0], {"seq": far})
    to_far.start()
    small_to_beside.wait()
    small[...] += small_seq[0]
    small_to_far.start()
    near_out[0] = summed(beside).astype(BF16)
    to_beside(0).start()
    total[...] = summed(seq_me)
    to_beside(0).wait_recv()
    total[...] += near_in[0].astype(F32)
    to_far.wait_recv()
    total[...] += far_in[...].astype(F32)
    small_to_far.wait()
    small[...] += small_seq[1]
    q_sum[...] = total[:rows]
    out_sum[...] = jnp.transpose(total[rows : 2 * rows])
    for i in range(per_line):
        kv_sum[i * lines : (i + 1) * lines] = total[2 * rows :, i * kv_width : (i + 1) * kv_width]
    for b in order:
        for k in range(len(dp_others)):
            to_dp(k, b).wait_send()
    to_beside(0).wait_send()
    to_beside(1).wait_send()
    to_far.wait_send()


def sum_last(number, q_part, kv_part, out_part, earlier, summed_all, summed_local):
    n_dp, n_seq, rows, width = q_part.shape
    kv_rows, kv_width = kv_part.shape[3:]
    block = (2 * rows + kv_rows * kv_width // width, width)
    n_far = n_dp - 1
    dma = pltpu.SemaphoreType.DMA
    vmem = pl.BlockSpec(memory_space=pltpu.VMEM)
    lanes = summed_all[0].shape[1]
    return pl.pallas_call(
        functools.partial(last_kernel, len(summed_all), len(summed_local)),
        out_shape=(
            jax.ShapeDtypeStruct((rows, width), F32),
            jax.ShapeDtypeStruct((kv_rows, kv_width), F32),
            jax.ShapeDtypeStruct((width, rows), F32),
            jax.ShapeDtypeStruct((16, lanes), F32),
        ),
        in_specs=[vmem] * 3 + anywhere(1) + [vmem] * (len(summed_all) + len(summed_local)),
        out_specs=(vmem,) * 4,
        scratch_shapes=[
            pltpu.VMEM((n_dp, n_seq) + block, BF16),
            pltpu.VMEM((n_far, n_seq) + block, BF16),
            pltpu.VMEM((2,) + block, BF16),
            pltpu.VMEM((2,) + block, BF16),
            pltpu.VMEM(block, BF16),
            pltpu.VMEM(block, BF16),
            pltpu.VMEM(block, F32),
            pltpu.VMEM((8, lanes), F32),
            pltpu.VMEM((8, lanes), F32),
            pltpu.VMEM((n_far, 16, lanes), F32),
            pltpu.VMEM((2, 16, lanes), F32),
            dma((n_far, n_seq)),
            dma((n_far, n_seq)),
            dma((2,)),
            dma((2,)),
            dma((1,)),
            dma((1,)),
            dma((4 + n_far,)),
            dma((4 + n_far,)),
        ],
        compiler_params=pltpu.CompilerParams(
            collective_id=number, has_side_effects=True, vmem_limit_bytes=48 * 1024 * 1024
        ),
        cost_estimate=estimate(70),
        name="sum_last",
    )(q_part, kv_part, out_part, earlier, *summed_all, *summed_local)


def shards(
    layer_input,
    lengths,
    cotangent,
    ln1_gain,
    ln1_bias,
    w_query,
    b_query,
    w_kv,
    b_value,
    w_out,
    b_out,
    ln2_gain,
    ln2_bias,
    w_up,
    b_up,
    w_down,
    b_down,
):
    n_rows, seq_len, model_width = layer_input.shape
    n_tensor = lax.axis_size("tensor")
    n_dp = lax.axis_size("dp")
    n_seq = lax.axis_size("seq")
    share_len = seq_len // n_tensor
    tensor_index = lax.axis_index("tensor")
    seq_index = lax.axis_index("seq")
    head_size = w_kv.shape[1] // 2
    num_heads = w_query.shape[1] // head_size
    q_scale = 1.0 / math.sqrt(head_size)
    n_tok = n_rows * seq_len
    n_own = n_rows * share_len

    def by_share(values_in):
        return jnp.moveaxis(values_in.reshape((n_rows, n_tensor, share_len) + values_in.shape[2:]), 1, 0)

    def own_share(values_in):
        return lax.dynamic_index_in_dim(values_in.reshape((n_tensor, n_own) + values_in.shape[1:]), tensor_index, 0, False)

    positions = seq_index * seq_len + jnp.arange(seq_len, dtype=jnp.int32)
    is_valid = (positions[None, :] < lengths[:, None]).astype(F32)
    valid_own = own_share(by_share(is_valid).reshape(n_tok))[:, None]
    grad_y_own = cotangent.reshape(n_own, model_width).astype(F32) * valid_own
    x_float = lax.optimization_barrier(by_share(layer_input).reshape(n_tok, model_width)).astype(F32)
    normed_x1, inv_one = normalize(x_float)
    flat_one = (normed_x1 * ln1_gain + ln1_bias).astype(BF16)
    kv_bias = jnp.concatenate([jnp.zeros((head_size,), F32), b_value.astype(F32)])
    kv_own = (jnp.dot(own_share(flat_one), w_kv, preferred_element_type=F32) + kv_bias).astype(BF16)
    queries = ((jnp.dot(flat_one, w_query, preferred_element_type=F32) + b_query) * q_scale).astype(BF16)
    grad_y_low, kv_all = front(0, grad_y_own.astype(BF16), kv_own)

    half_width = model_width // n_dp
    hidden = w_up.shape[1]
    dp_me = lax.axis_index("dp")

    first_rows = n_tok * 5 // 128 * 16
    mixed_heads, log_total = attention(lengths, queries, kv_all)
    attn_own, grad_y_far_a = product_to_owners(
        "attn_out", 1, mixed_heads, w_out, False, (grad_y_low,), ((0, 0, first_rows, None, half_width),)
    )
    x_own = own_share(x_float)
    resid_own = x_own + (attn_own + b_out)
    normed_x2, inv_two = normalize(resid_own)
    normed_two = (normed_x2 * ln2_gain + ln2_bias).astype(BF16)
    flat_two, grad_y_far_b, two_far_own = gather_shares(
        "gather_norm_two",
        2,
        normed_two,
        (grad_y_low, normed_two),
        ((0, first_rows, n_tok - first_rows, None, half_width), (1, 0, n_own, None, half_width)),
    )
    pre_act = jnp.dot(flat_two, w_up, preferred_element_type=F32) + b_up
    activated, gelu_pull = jax.vjp(lambda inner_in: jax.nn.gelu(inner_in, approximate=True), pre_act)
    act_low = activated.astype(BF16)
    grad_act = times_transposed(grad_y_low, w_down)
    grad_pre = gelu_pull(grad_act)[0].astype(BF16)

    def mine(ref):
        return ref.at[:, pl.ds(pl.multiple_of(lax.axis_index("dp") * half_width, half_width), half_width)]

    def tokens_of(ref, k, first=0, rows=n_tok):
        return ref.at[pl.ds((k + 1) * n_tok + first, rows)]

    group = hidden * 3 // 8
    half_hidden = hidden // 2

    def part_down(first, width):
        def views(refs, left, right):
            act, grads, grads_far_a, grads_far_b = refs
            pairs = [(act.at[:, pl.ds(first, width)], tokens_of(left, -1)), (mine(grads), tokens_of(right, -1))]
            for k in range(n_dp - 1):
                pairs.append((grads_far_a.at[k], tokens_of(right, k, 0, first_rows)))
                pairs.append((grads_far_b.at[k], tokens_of(right, k, first_rows, n_tok - first_rows)))
            return pairs

        arrays = (act_low, grad_y_low, grad_y_far_a, grad_y_far_b)
        return Guest(arrays, views, (n_dp * n_tok, width), (n_dp * n_tok, half_width), True, (0, first))

    def part_up(first, width):
        def views(refs, left, right):
            two, far_two, pre = refs
            pairs = [(mine(two), tokens_of(left, -1)), (pre.at[:, pl.ds(first, width)], tokens_of(right, -1))]
            for k in range(n_dp - 1):
                pairs.append((far_two.at[:, pl.ds(k * half_width, half_width)], tokens_of(left, k)))
            return pairs

        arrays = (flat_two, two_far, grad_pre)
        return Guest(arrays, views, (n_dp * n_tok, half_width), (n_dp * n_tok, width), False, (2, first))

    def over_seq(values_in):
        return lax.psum_scatter(values_in, "seq", scatter_dimension=0, tiled=True)

    grad_n2, down_a = product_to_owners("grad_norm_two", 3, grad_pre, w_up, True, guest=part_down(0, group))
    down_a = over_seq(down_a)
    grad_resid = grad_y_own + norm_back(grad_n2, normed_x2, inv_two, ln2_gain)
    grad_resid_low = grad_resid.astype(BF16)
    flat_resid, down_b = gather_shares("gather_grad_resid", 4, grad_resid_low, guest=part_down(group, group))
    down_b = over_seq(down_b)
    grad_mixed = times_transposed(flat_resid, w_out).astype(BF16)
    flat_query, grad_kv = attention_back(lengths, queries, grad_mixed, kv_all, log_total)
    two_swapped = jnp.swapaxes(two_far_own, 0, 1).reshape(n_own, -1)
    grad_n1, two_far, down_c = product_to_owners(
        "grad_norm_one",
        6,
        flat_query,
        w_query,
        True,
        (down_a,),
        guest=part_down(2 * group, hidden - 2 * group),
        spread=two_swapped,
    )
    down_c = over_seq(down_c)
    grad_n1 = grad_n1 * q_scale
    two_far = two_far.reshape(n_tok, (n_dp - 1) * half_width)
    flat_kv, up_a = sum_grad_kv(7, grad_kv, (down_b,), (), part_up(0, half_hidden))
    up_a = over_seq(up_a)
    mlp_raw, up_b = product_to_owners(
        "mlp_out", 5, act_low, w_down, False, (flat_kv, down_c), guest=part_up(half_hidden, half_hidden)
    )
    up_b = over_seq(up_b)
    mlp_own = mlp_raw + b_down
    g_w_down = jnp.concatenate([down_a, down_b, down_c], 0).astype(F32)
    g_w_up = jnp.concatenate([up_a, up_b], 1).astype(F32)

    def by_owner(values_in, *between):
        return values_in.astype(BF16).reshape((n_dp, n_seq) + between + (-1, values_in.shape[1]))

    q_part = by_owner(across_rows(flat_one, flat_query) * q_scale)
    kv_part = by_owner(across_rows(flat_one, flat_kv), n_tensor)
    out_part = by_owner(across_rows(flat_resid, mixed_heads))
    y_own = (valid_own * (resid_own + mlp_own)).astype(BF16).reshape(n_rows, share_len, model_width)

    own_kv = own_share(flat_kv)
    grad_n1 = grad_n1 + times_transposed(own_kv, w_kv)
    normed_x1_own = own_share(normed_x1)
    x_grad_own = grad_resid + norm_back(grad_n1, normed_x1_own, own_share(inv_one), ln1_gain)
    x_grad_own = x_grad_own.reshape(n_rows, share_len, model_width)
    def token_sum(values_in):
        return jnp.sum(values_in.astype(F32), axis=0, keepdims=True)

    over_all = [
        token_sum(grad_n1 * normed_x1_own),
        token_sum(grad_n1),
        token_sum(grad_n2 * normed_x2),
        token_sum(grad_n2),
        token_sum(grad_resid_low),
        token_sum(grad_y_own),
        token_sum(own_kv[:, head_size:]),
    ]
    over_local = [token_sum(grad_pre), token_sum(flat_query) * q_scale]
    g_w_query, g_w_kv, g_w_out, small = sum_last(9, q_part, kv_part, out_part, up_a, over_all, over_local)
    owners = n_dp * n_seq
    owner = dp_me * n_seq + seq_index
    last_owner = owner * n_tensor + tensor_index

    def owned(values_in, index, count):
        width = values_in.shape[-1] // count
        return lax.dynamic_slice_in_dim(values_in, index * width, width, values_in.ndim - 1)

    query_out = owned(small[9, : num_heads * head_size].reshape(num_heads, head_size), owner, owners)
    up_out = owned(small[8].reshape(-1, 128), owner, owners)
    small_out = owned(small[:6], last_owner, owners * n_tensor)
    value_out = owned(small[6, :head_size], last_owner, owners * n_tensor)
    return (
        y_own,
        x_grad_own,
        g_w_query,
        query_out,
        g_w_kv,
        value_out,
        g_w_out,
        g_w_up,
        up_out,
        g_w_down,
        small_out,
    )


def solution(mesh):
    placed = (
        P("dp", "seq", None),
        P("dp"),
        P("dp", ("seq", "tensor"), None),
        P(),
        P(),
        P(None, "tensor"),
        P("tensor"),
        P(),
        P(),
        P("tensor", None),
        P(),
        P(),
        P(),
        P(None, "tensor"),
        P("tensor"),
        P("tensor", None),
        P(),
    )
    return jax.shard_map(
        shards,
        mesh=mesh,
        in_specs=placed,
        out_specs=(
            P("dp", ("seq", "tensor"), None),
            P("dp", ("seq", "tensor"), None),
            P(("dp", "seq"), "tensor"),
            P("tensor", ("dp", "seq")),
            P(("dp", "seq", "tensor"), None),
            P(("dp", "seq", "tensor")),
            P("tensor", ("dp", "seq")),
            P(("dp", "seq"), "tensor"),
            P("tensor", ("dp", "seq")),
            P("tensor", ("dp", "seq")),
            P(None, ("dp", "seq", "tensor")),
        ),
        check_vma=False,
    )
```
